32 devices in a mesh: groups: 2 (over x), ctx: 16 (over z, y, core).
Axes of the slice: x: 2, y: 2, z: 4, core: 2. Of those that a mesh axis runs over, the one named last changes fastest.
Arguments:
- hidden: bfloat16 [4096, 2048], P(('groups', 'ctx')), parts along dimension 0, may hold values from -6 to 6
- w_query: bfloat16 [2048, 2048], P('ctx')
- w_keyval: bfloat16 [2048, 1024], P('ctx')
- w_out: bfloat16 [2048, 2048], P('ctx'), may hold values from -1.796875 to 1.796875
- global_blocks: int32 [4], P('groups'), parts along dimension 0, may hold values from 0 to 15, as said below
- cotangent: bfloat16 [4096, 2048], P(('groups', 'ctx')), parts along dimension 0, may hold values from -6 to 6
Outputs:
- combined: bfloat16 [4096, 2048], P(('groups', 'ctx')), parts along dimension 0
- input_grad: bfloat16 [4096, 2048], P(('groups', 'ctx')), parts along dimension 0
The draws below stay inside these ranges and needn't reach their ends.
There are 2 independent parts, one for each index of `groups`. The reference program is written for one: setup_inputs(seed, part) draws one part's arguments, and reference() takes and returns one part's arrays. A program takes and returns all parts, laid end to end along the dimension named above; an argument that names none is the same for every part. Nothing has to cross between parts.
Inputs may be any that keep to these rules, and one draw needn't show every extreme that they name: `global_blocks`: 2 distinct block indices; the last block, 15, is always one of them, at a position drawn from the seed.
All inputs are finite; a program needn't handle non-finite values.
Results may differ from the reference program's by a relative error of at most 0.0098.
Values may be sent and summed in bfloat16 or wider, within the bound.
No kernel may reach another device: no remote copies, remote signals or barrier semaphores. Data moves between devices by JAX's collectives and lax.ppermute only.
A program may use at most 128 MiB of HBM per device.

```python
import jax
import jax.numpy as jnp
from jax import lax

D = 2048
HEADS = 16
KVH = 4
HDIM = 128
BLK = 128
GLOBALS = 2
TOKENS = 2048
NBLK = 16


def tied_keys(key):
    return jax.random.normal(jax.random.fold_in(key, 11), (D, KVH * HDIM), jnp.float32) * D ** (-0.5)


def draw_w_keyval(key, part):
    key_part = tied_keys(key)
    value_part = jax.random.normal(jax.random.fold_in(key, 12), (D, KVH * HDIM), jnp.float32) * D ** (-0.5)
    return jnp.concatenate([key_part, value_part], axis=1).astype(jnp.bfloat16)


def draw_w_query(key, part):
    own_part = jax.random.normal(jax.random.fold_in(key, 14), (D, HEADS * HDIM), jnp.float32) * D ** (-0.5)
    return own_part.astype(jnp.bfloat16)


def draw_global_blocks(key, part):
    others = jax.random.permutation(jax.random.fold_in(key, 21), NBLK - 1)[:GLOBALS - 1].astype(jnp.int32)
    chosen = jnp.concatenate([others, jnp.full((1,), NBLK - 1, jnp.int32)])
    order = jax.random.permutation(jax.random.fold_in(key, 22), GLOBALS)
    return chosen[order].astype(jnp.int32)


def levels(key, dims, cuts, low, top_value):
    def one(dim, blocks):
        steps = jax.random.uniform(jax.random.fold_in(jax.random.fold_in(key, 6), dim), (blocks,), jnp.float32, low / len(cuts), top_value / len(cuts))
        return jnp.repeat(jnp.exp(steps), dims[dim] // blocks).reshape((-1,) + (1,) * (len(dims) - dim - 1))

    factor_of = one(*cuts[0])
    for cut in cuts[1:]:
        factor_of = factor_of * one(*cut)
    return factor_of


def gaussian(key, dims, deviation, reach, split=(), kind=jnp.bfloat16):
    array = jax.random.normal(key, dims, jnp.float32) * deviation
    if len(split) > 0:
        array = levels(key, dims, split, -0.22, 0.18) * array
    return jnp.clip(array, min=-reach, max=reach).astype(kind)


def setup_inputs(seed: int = 0, part: int = 0) -> dict:
    splits = jax.random.split(jax.random.key(seed), 7)
    part_splits = jax.random.split(jax.random.fold_in(splits[6], part), 7)
    hidden = gaussian(part_splits[0], (TOKENS, D), 1.0, 6.0, ((0, 16),))
    w_query = draw_w_query(jax.random.fold_in(splits[6], 71), part)
    w_keyval = draw_w_keyval(jax.random.fold_in(splits[6], 71), part)
    w_out = gaussian(splits[3], (HEADS * HDIM, D), 0.3, 1.796875, ((0, 16),))
    global_blocks = draw_global_blocks(jax.random.fold_in(jax.random.fold_in(splits[6], part), 71), part)
    cotangent = gaussian(part_splits[5], (TOKENS, D), 1.0, 6.0, ((0, 16),))
    return dict(hidden=hidden, w_query=w_query, w_keyval=w_keyval, w_out=w_out, global_blocks=global_blocks, cotangent=cotangent)


epsilon = 1e-05

def normalize(values):
    widened = values.astype(jnp.float32)
    inv_rms = lax.rsqrt(lax.optimization_barrier(jnp.mean(widened * widened, axis=1, keepdims=True)) + epsilon)
    return (widened * inv_rms, inv_rms)

def rounded(values):
    return lax.optimization_barrier(values.astype(jnp.bfloat16)).astype(jnp.float32)

def key_set(kv_blocks, block, global_blocks):
    previous = jnp.maximum(block - 1, 0)
    chosen = jnp.concatenate([jnp.stack([previous, block]).astype(jnp.int32), global_blocks.astype(jnp.int32)])
    key_rows = kv_blocks[chosen].reshape((2 + GLOBALS) * BLK, kv_blocks.shape[2])
    key_flags = jnp.concatenate([jnp.stack([block >= 1, block >= 0]), (global_blocks != block) & (global_blocks != block - 1)])
    return (chosen, key_rows, jnp.repeat(key_flags, BLK))

def probabilities(query_rows, key_rows, validity):
    query = query_rows.astype(jnp.float32).reshape(BLK, KVH, HEADS // KVH, HDIM)
    keys_only = key_rows[:, :KVH * HDIM].astype(jnp.float32).reshape(-1, KVH, HDIM)
    scores = jnp.einsum('qgrd,kgd->grqk', query, keys_only) * HDIM ** (-0.5)
    scores = jnp.where(validity, scores, -jnp.inf)
    exponent = jnp.exp(scores - lax.optimization_barrier(jnp.max(scores, axis=-1, keepdims=True)))
    return exponent / lax.optimization_barrier(jnp.sum(exponent, axis=-1, keepdims=True))

def branch_forward(inputs, w_query, w_keyval, w_out, global_blocks):
    scaled, inv_rms = normalize(inputs)
    normed = scaled.astype(jnp.bfloat16)
    queries = jnp.dot(normed, w_query, preferred_element_type=jnp.float32).astype(jnp.bfloat16)
    keyvals = jnp.dot(normed, w_keyval, preferred_element_type=jnp.float32).astype(jnp.bfloat16)
    kv_blocks = keyvals.reshape(NBLK, BLK, keyvals.shape[1])
    query_blocks = queries.reshape(NBLK, BLK, queries.shape[1])

    def attend_block(block):
        chosen, key_rows, validity = key_set(kv_blocks, block, global_blocks)
        prob_full = probabilities(query_blocks[block], key_rows, validity)
        values_only = key_rows[:, KVH * HDIM:].astype(jnp.float32).reshape(-1, KVH, HDIM)
        attended = jnp.einsum('grqk,kgd->qgrd', rounded(prob_full), values_only)
        return attended.reshape(BLK, HEADS * HDIM).astype(jnp.bfloat16)
    attended = lax.map(attend_block, jnp.arange(NBLK, dtype=jnp.int32)).reshape(TOKENS, HEADS * HDIM)
    outputs = jnp.dot(attended, w_out, preferred_element_type=jnp.float32)
    return (outputs, (scaled, inv_rms, kv_blocks, query_blocks))

def branch_backward(grad_rows, saved, w_query, w_keyval, w_out, global_blocks):
    scaled, inv_rms, kv_blocks, query_blocks = saved
    grad_att = jnp.dot(grad_rows, w_out.T, preferred_element_type=jnp.float32).astype(jnp.bfloat16)
    grad_blocks = grad_att.reshape(NBLK, BLK, HEADS * HDIM)

    def step(carry, block):
        chosen, key_rows, validity = key_set(kv_blocks, block, global_blocks)
        prob_full = probabilities(query_blocks[block], key_rows, validity)
        prob_half = rounded(prob_full)
        keys_only = key_rows[:, :KVH * HDIM].astype(jnp.float32).reshape(-1, KVH, HDIM)
        values_only = key_rows[:, KVH * HDIM:].astype(jnp.float32).reshape(-1, KVH, HDIM)
        query = query_blocks[block].astype(jnp.float32).reshape(BLK, KVH, HEADS // KVH, HDIM)
        upstream = grad_blocks[block].astype(jnp.float32).reshape(BLK, KVH, HEADS // KVH, HDIM)
        grad_prob = jnp.einsum('qgrd,kgd->grqk', upstream, values_only)
        center = lax.optimization_barrier(jnp.sum(prob_full * grad_prob, axis=-1, keepdims=True))
        grad_score = rounded(prob_full * (grad_prob - center) * HDIM ** (-0.5))
        grad_query = jnp.einsum('grqk,kgd->qgrd', grad_score, keys_only).reshape(BLK, HEADS * HDIM).astype(jnp.bfloat16)
        grad_keys = jnp.einsum('grqk,qgrd->kgd', grad_score, query).reshape(-1, KVH * HDIM)
        grad_values = jnp.einsum('grqk,qgrd->kgd', prob_half, upstream).reshape(-1, KVH * HDIM)
        terms = jnp.concatenate([grad_keys, grad_values], axis=1).reshape(2 + GLOBALS, BLK, 2 * KVH * HDIM)
        return (carry.at[chosen].add(terms), grad_query)
    initial = jnp.zeros((NBLK, BLK, 2 * KVH * HDIM), jnp.float32)
    kv_grads, grad_queries = lax.scan(step, initial, jnp.arange(NBLK, dtype=jnp.int32))
    key_grads = kv_grads.reshape(TOKENS, 2 * KVH * HDIM).astype(jnp.bfloat16)
    grad_norm = jnp.dot(grad_queries.reshape(TOKENS, HEADS * HDIM), w_query.T, preferred_element_type=jnp.float32)
    grad_norm = grad_norm + jnp.dot(key_grads, w_keyval.T, preferred_element_type=jnp.float32)
    return inv_rms * (grad_norm - scaled * lax.optimization_barrier(jnp.mean(grad_norm * scaled, axis=1, keepdims=True)))

def reference(hidden, w_query, w_keyval, w_out, global_blocks, cotangent):
    mirrored = hidden[::-1, ::-1]
    plain_out, plain_saved = branch_forward(hidden, w_query, w_keyval, w_out, global_blocks)
    mirror_out, mirror_saved = branch_forward(mirrored, w_query, w_keyval, w_out, global_blocks)
    combined = (plain_out + mirror_out[::-1]).astype(jnp.bfloat16)
    plain_grad = branch_backward(cotangent, plain_saved, w_query, w_keyval, w_out, global_blocks)
    mirror_grad = branch_backward(cotangent[::-1], mirror_saved, w_query, w_keyval, w_out, global_blocks)
    input_grad = (plain_grad + mirror_grad[::-1, ::-1]).astype(jnp.bfloat16)
    return (combined, input_grad)
```

```python
import jax
import jax.numpy as jnp
from jax import lax
from jax.experimental import pallas as pl
from jax.experimental.pallas import tpu as pltpu
from jax.sharding import Mesh, PartitionSpec as P

HEADS = 16
KVH = 4
HDIM = 128
BLK = 128
REP = HEADS // KVH
EPS = 1e-05
SCALE = HDIM ** (-0.5)
F32 = jnp.float32
BF16 = jnp.bfloat16
VMEM = 56 * 1024 * 1024


def dot(a, b, ca, cb):
    return lax.dot_general(a, b, (((ca,), (cb,)), ((), ())), preferred_element_type=F32)


def flip_matrix(n):
    i = lax.broadcasted_iota(jnp.int32, (n, n), 0)
    j = lax.broadcasted_iota(jnp.int32, (n, n), 1)
    return jnp.where(i + j == n - 1, 1.0, 0.0).astype(BF16)


def params():
    return pltpu.CompilerParams(vmem_limit_bytes=VMEM)


def whole():
    return pl.BlockSpec(memory_space=pltpu.VMEM)


def smem():
    return pl.BlockSpec(memory_space=pltpu.SMEM)


def norm_kernel(info, h00, h01, h10, h11, out):
    core = info[0]
    flip = flip_matrix(128)
    for side, refs in enumerate(((h00, h01), (h10, h11))):
        place = core if side == 0 else 1 - core
        for grp in range(2):
            u = refs[grp][...].astype(F32)
            inv = lax.rsqrt(jnp.mean(u * u, axis=1, keepdims=True) + EPS)
            n = (u * inv).astype(BF16)
            row = pl.multiple_of(place * (2 * BLK) + grp * BLK, BLK)
            out[0, pl.ds(row, BLK), :] = n
            count = n.shape[1] // 128
            for k in range(count):
                m = count - 1 - k
                out[1, pl.ds(row, BLK), m * 128 : m * 128 + 128] = dot(
                    n[:, k * 128 : k * 128 + 128], flip, 1, 0
                ).astype(BF16)


def grad_att_kernel(info, c00, c01, c10, c11, w, out):
    core = info[0]
    for side, refs in enumerate(((c00, c01), (c10, c11))):
        place = core if side == 0 else 1 - core
        rows = jnp.concatenate([refs[0][...], refs[1][...]], axis=0)
        row = pl.multiple_of(place * (2 * BLK), 2 * BLK)
        out[pl.ds(row, 2 * BLK), :] = dot(rows, w[...], 1, 1).astype(BF16)


def attention_kernel(info, q, ga, kv, halo, static, dyn, att, gq, dkv, dhalo, dstatic, ddyn):
    last = info[2] - 1
    t = info[1]
    g_dyn = info[3 + pl.program_id(0)]
    for strand in range(2):
        sets = [kv[strand, 0, 0], kv[strand, 1, 0], halo[strand, 0], static[strand, 0], dyn[strand, 0]]
        stat_block = last if strand == 0 else 0
        dyn_block = g_dyn if strand == 0 else last - g_dyn
        sums = [None] * 5
        for side in range(2):
            block = 2 * t + side
            near = block - 1 if strand == 0 else block + 1
            if strand == 0:
                near_set = 2 if side == 0 else 0
            else:
                near_set = 1 if side == 0 else 2
            order = (near_set, side, 3, 4)
            flags = (
                (near >= 0) & (near <= last),
                None,
                (stat_block != block) & (stat_block != near),
                (dyn_block != block) & (dyn_block != near),
            )
            keys = jnp.concatenate([sets[i][:, :HDIM] for i in order], axis=0)
            values = jnp.concatenate([sets[i][:, HDIM:] for i in order], axis=0)
            qs = q[strand, side, 0]
            gs = ga[side, 0]
            rows = jnp.concatenate([qs[:, i * HDIM : (i + 1) * HDIM] for i in range(REP)], axis=0)
            ups = jnp.concatenate([gs[:, i * HDIM : (i + 1) * HDIM] for i in range(REP)], axis=0)
            s = dot(rows, keys, 1, 1) * SCALE
            parts = []
            for i in range(4):
                part = s[:, i * BLK : (i + 1) * BLK]
                if flags[i] is not None:
                    part = jnp.where(flags[i], part, -jnp.inf)
                parts.append(part)
            s = jnp.concatenate(parts, axis=1)
            e = jnp.exp(s - jnp.max(s, axis=1, keepdims=True))
            p = e * (1.0 / jnp.sum(e, axis=1, keepdims=True))
            ph = p.astype(BF16)
            o = dot(ph, values, 1, 0)
            dp = dot(ups, values, 1, 1)
            center = jnp.sum(p * dp, axis=1, keepdims=True)
            ds = (p * (dp - center) * SCALE).astype(BF16)
            dq = dot(ds, keys, 1, 0)
            dk = dot(ds, rows, 0, 0)
            dv = dot(ph, ups, 0, 0)
            for i in range(REP):
                att[strand, side, 0, :, i * HDIM : (i + 1) * HDIM] = o[i * BLK : (i + 1) * BLK].astype(BF16)
                gq[strand, side, 0, :, i * HDIM : (i + 1) * HDIM] = dq[i * BLK : (i + 1) * BLK].astype(BF16)
            for i in range(4):
                term = (dk[i * BLK : (i + 1) * BLK], dv[i * BLK : (i + 1) * BLK])
                old = sums[order[i]]
                sums[order[i]] = term if old is None else (old[0] + term[0], old[1] + term[1])
        targets = (dkv.at[strand, 0, 0], dkv.at[strand, 1, 0], dhalo.at[strand, 0], dstatic.at[strand, 0], ddyn.at[strand, 0])
        for target, (dk, dv) in zip(targets, sums):
            target[:, :HDIM] = dk.astype(target.dtype)
            target[:, HDIM:] = dv.astype(target.dtype)


def output_kernel(info, att, w, keep, send):
    core = info[0]
    for target, place in ((keep, core), (send, 1 - core)):
        total = dot(att[0, place], w[...], 1, 0) + dot(att[1, place], w[...], 1, 0)
        target[...] = total.astype(target.dtype)


def grad_norm_kernel(info, gq, dkv, halo, static, dyn, wq, wkv, wqm, wkvm, keep, send, kg):
    core = info[0]
    t = info[1]
    blocks = info[2]
    last = blocks - 1

    @pl.when(pl.program_id(0) == 0)
    def _():
        for strand in range(2):
            stat_block = last if strand == 0 else 0
            for side in range(2):
                for grp in range(2):
                    total = dkv[strand, side, grp]
                    if side != strand:
                        total = total + halo[strand, grp].astype(F32)
                        total = total + jnp.where(2 * t + side == stat_block, static[strand, grp].astype(F32), 0.0)
                    dyn_block = info[3 + grp] if strand == 0 else last - info[3 + grp]
                    total = total + jnp.where(2 * t + side == dyn_block, dyn[strand, grp].astype(F32), 0.0)
                    kg[strand, side, grp * BLK : (grp + 1) * BLK, :] = total.astype(BF16)

    width = wq.shape[0]
    flip = flip_matrix(width)
    wqf = dot(flip, wqm[...], 1, 0).astype(BF16)
    wkvf = dot(flip, wkvm[...], 1, 0).astype(BF16)
    for target, place in ((keep, core), (send, 1 - core)):
        total = dot(gq[0, place], wq[...], 1, 1) + dot(kg[0, place], wkv[...], 1, 1)
        total = total + dot(gq[1, place], wqf, 1, 1) + dot(kg[1, place], wkvf, 1, 1)
        target[...] = total.astype(target.dtype)


def swap(value, axis):
    return lax.ppermute(value, axis, [(0, 1), (1, 0)])


def pair(own, other, index):
    return jnp.where(index == 0, jnp.concatenate([own, other], 0), jnp.concatenate([other, own], 0))


def ring(value, axis):
    count = lax.axis_size(axis)
    return lax.ppermute(value, axis, [(i, (i + 1) % count) for i in range(count)])


def gather_rows(chunk):
    na, nb = lax.axis_size("a"), lax.axis_size("b")
    a, b = lax.axis_index("a"), lax.axis_index("b")
    size = chunk.shape[0]
    pieces = []
    for step in range(na):
        inner = chunk
        for turn in range(nb):
            pos = ((a - step) % na) * nb + (b - turn) % nb
            pieces.append((pos, inner))
            if turn + 1 < nb:
                inner = ring(inner, "b")
        if step + 1 < na:
            chunk = ring(chunk, "a")
    full = jnp.zeros((na * nb * size, chunk.shape[1]), chunk.dtype)
    for pos, piece in pieces:
        full = lax.dynamic_update_slice(full, piece, (pos * size, 0))
    return full


def output_rows(w_out, x, a, b, c):
    na, nb = lax.axis_size("a"), lax.axis_size("b")
    mine = 2 * x + c
    if (na, nb) != (4, 2):
        full = lax.all_gather(w_out, ("a", "b", "c"), axis=0, tiled=True)
        return lax.dynamic_slice(full, (mine * REP * HDIM, 0), (REP * HDIM, full.shape[1]))
    source = pair(w_out, swap(w_out, "c"), c)
    current = jnp.where(a == mine, source, 0).astype(source.dtype)

    def spot(x, a, c):
        return (x * na + a) * 2 + c

    def send(value, moves):
        pairs = []
        for (sx, sc), links in moves.items():
            pairs += [(spot(sx, i, sc), spot(sx, j, sc)) for i, j in links]
        return lax.ppermute(value, ("x", "a", "c"), pairs)

    def across(value, holders):
        pairs = []
        for (sx, sc), levels in holders.items():
            for i in levels:
                at = (sx * na + i) * 4 + sc
                pairs += [(at, at + 2), (at + 2, at)]
        return lax.ppermute(value, ("x", "a", "b", "c"), pairs)

    first = {(0, 0): [(0, 1)], (0, 1): [(1, 2)], (1, 0): [(2, 1)], (1, 1): [(3, 2)]}
    second = {(0, 0): [(0, 2), (1, 3)], (0, 1): [(1, 0), (2, 3)], (1, 0): [(2, 3), (1, 0)], (1, 1): [(3, 1), (2, 0)]}
    other = across(current, {(0, 0): [0], (0, 1): [1], (1, 0): [2], (1, 1): [3]})
    got = send(current, first)
    other = other + across(got, {k: [j for _, j in v] for k, v in first.items()})
    current = current + got
    got = send(current, second)
    other = other + across(got, {k: [j for _, j in v] for k, v in second.items()})
    current = current + got
    return pair(current, other, b)


def exchange_bits(index, axis):
    count = lax.axis_size(axis)
    bit = 1
    while bit < count:
        yield (index // bit) % 2, [(i, i ^ bit) for i in range(count)]
        bit *= 2


def body(hidden, w_query, w_keyval, w_out, global_blocks, cotangent):
    x, a, b, c = (lax.axis_index(n) for n in ("x", "a", "b", "c"))
    na, nb = lax.axis_size("a"), lax.axis_size("b")
    n = na * nb
    t = a * nb + b
    blocks = 2 * n
    width = hidden.shape[1]
    mine = 2 * x + c
    theirs = 2 * x + 1 - c
    line_up = [(i, i + 1) for i in range(n - 1)]
    line_down = [(i + 1, i) for i in range(n - 1)]

    g_own = jnp.sum(global_blocks) - (blocks - 1)
    g_own = jnp.reshape(g_own, (1,)).astype(jnp.int32)
    g_both = jnp.concatenate([g_own, swap(g_own, "x")])
    info = jnp.concatenate([jnp.stack([c, t, jnp.int32(blocks)]).astype(jnp.int32), g_both])

    h10 = swap(hidden, "c")
    h01 = swap(hidden, "x")
    h11 = swap(h01, "c")

    half = KVH * HDIM

    def kv_columns(j):
        return jnp.concatenate(
            [
                lax.dynamic_slice_in_dim(w_keyval, j * HDIM, HDIM, 1),
                lax.dynamic_slice_in_dim(w_keyval, half + j * HDIM, HDIM, 1),
            ],
            axis=1,
        )

    def q_columns(j):
        return lax.dynamic_slice_in_dim(w_query, j * REP * HDIM, REP * HDIM, 1)

    kv_weight = gather_rows(pair(kv_columns(mine), swap(kv_columns(theirs), "c"), c))
    normed = pl.pallas_call(
        norm_kernel,
        out_shape=jax.ShapeDtypeStruct((2, 4 * BLK, width), BF16),
        in_specs=[smem()] + [whole()] * 4,
        out_specs=whole(),
        compiler_params=params(),
        name="norm",
    )(info, hidden, h01, h10, h11)
    normed = normed.reshape(8 * BLK, width)
    kv = dot(normed, kv_weight, 1, 0).astype(BF16).reshape(2, 2, 2, BLK, 2 * HDIM)

    ctx = ("a", "b")
    up = kv[0, 1]
    down = kv[1, 0]
    halo = jnp.stack([lax.ppermute(up, ctx, line_up), lax.ppermute(down, ctx, line_down)])
    dyn_plain = g_both
    dyn_blocks = jnp.stack([dyn_plain, blocks - 1 - dyn_plain])
    dyn_side = (dyn_blocks % 2)[:, :, None, None]
    dyn_own = (dyn_blocks // 2 == t)[:, :, None, None]
    dyn = jnp.where(dyn_own, jnp.where(dyn_side == 0, kv[:, 0], kv[:, 1]), 0).astype(BF16)
    upper = jnp.where(t == n - 1, up, 0).astype(BF16)
    lower = jnp.where(t == 0, down, 0).astype(BF16)
    for index, axis in ((b, "b"), (a, "a")):
        for bit, pairs in exchange_bits(index, axis):
            packed = jnp.concatenate([dyn, jnp.where(bit == 1, upper, lower)[None]], axis=0)
            got = lax.ppermute(packed, axis, pairs)
            dyn = dyn + got[:2]
            upper = jnp.where(bit == 0, upper + got[2], upper)
            lower = jnp.where(bit == 1, lower + got[2], lower)
    static = jnp.stack([upper, lower])

    q_weight = gather_rows(pair(q_columns(mine), swap(q_columns(theirs), "c"), c))
    queries = dot(normed, q_weight, 1, 0).astype(BF16).reshape(2, 2, 2, BLK, REP * HDIM)

    c10 = swap(cotangent, "c")
    c01 = swap(cotangent, "x")
    c11 = swap(c01, "c")
    o_weight = output_rows(w_out, x, a, b, c)
    grad_att = pl.pallas_call(
        grad_att_kernel,
        out_shape=jax.ShapeDtypeStruct((4 * BLK, REP * HDIM), BF16),
        in_specs=[smem()] + [whole()] * 5,
        out_specs=whole(),
        compiler_params=params(),
        name="grad_att",
    )(info, cotangent, c01, c10, c11, o_weight)
    grad_att = grad_att.reshape(2, 2, BLK, REP * HDIM)

    wide = pl.BlockSpec((2, 2, 1, BLK, REP * HDIM), lambda g: (0, 0, g, 0, 0))
    pairs_spec = pl.BlockSpec((2, 2, 1, BLK, 2 * HDIM), lambda g: (0, 0, g, 0, 0))
    strand_spec = pl.BlockSpec((2, 1, BLK, 2 * HDIM), lambda g: (0, g, 0, 0))
    small = jax.ShapeDtypeStruct((2, 2, BLK, 2 * HDIM), BF16)
    att, gq, dkv, dhalo, dstatic, ddyn = pl.pallas_call(
        attention_kernel,
        grid=(2,),
        out_shape=(
            jax.ShapeDtypeStruct(queries.shape, BF16),
            jax.ShapeDtypeStruct(queries.shape, BF16),
            jax.ShapeDtypeStruct(kv.shape, F32),
            small,
            small,
            small,
        ),
        in_specs=[
            smem(),
            wide,
            pl.BlockSpec((2, 1, BLK, REP * HDIM), lambda g: (0, g, 0, 0)),
            pairs_spec,
            strand_spec,
            strand_spec,
            strand_spec,
        ],
        out_specs=(wide, wide, pairs_spec, strand_spec, strand_spec, strand_spec),
        compiler_params=params(),
        name="attention",
    )(info, queries, grad_att, kv, halo, static, dyn)

    halo_back = jnp.stack([lax.ppermute(dhalo[0], ctx, line_down), lax.ppermute(dhalo[1], ctx, line_up)])
    upper, lower = dstatic[0], dstatic[1]
    for index, axis in ((b, "b"), (a, "a")):
        for bit, pairs in exchange_bits(index, axis):
            packed = jnp.concatenate([ddyn, jnp.where(bit == 0, upper, lower)[None]], axis=0)
            got = lax.ppermute(packed, axis, pairs)
            ddyn = ddyn + got[:2]
            upper = jnp.where(bit == 1, upper + got[2], upper)
            lower = jnp.where(bit == 0, lower + got[2], lower)
    static_back = jnp.stack([upper, lower])

    rows = 2 * BLK

    def finish(keep, send):
        total = keep + swap(send, "c").astype(F32)
        return total[:BLK] + swap(total[BLK:].astype(BF16), "x").astype(F32)

    chunk = width // 4
    partial = (jax.ShapeDtypeStruct((rows, width), F32), jax.ShapeDtypeStruct((rows, width), BF16))
    combined = finish(
        *pl.pallas_call(
            output_kernel,
            grid=(width // chunk,),
            out_shape=partial,
            in_specs=[
                smem(),
                pl.BlockSpec((2, 2, rows, REP * HDIM), lambda k: (0, 0, 0, 0)),
                pl.BlockSpec((REP * HDIM, chunk), lambda k: (0, k)),
            ],
            out_specs=[pl.BlockSpec((rows, chunk), lambda k: (0, k))] * 2,
            compiler_params=params(),
            name="output",
        )(info, att.reshape(2, 2, rows, REP * HDIM), o_weight)
    ).astype(BF16)

    chunk = 256
    steps = width // chunk

    def fixed(shape):
        return pl.BlockSpec(shape, lambda k: (0,) * len(shape))

    keep, send = pl.pallas_call(
        grad_norm_kernel,
        grid=(steps,),
        out_shape=partial,
        in_specs=[
            smem(),
            fixed((2, 2, rows, REP * HDIM)),
            fixed(dkv.shape),
            fixed(small.shape),
            fixed(small.shape),
            fixed(small.shape),
            pl.BlockSpec((chunk, REP * HDIM), lambda k: (k, 0)),
            pl.BlockSpec((chunk, 2 * HDIM), lambda k: (k, 0)),
            pl.BlockSpec((chunk, REP * HDIM), lambda k: (steps - 1 - k, 0)),
            pl.BlockSpec((chunk, 2 * HDIM), lambda k: (steps - 1 - k, 0)),
        ],
        out_specs=[pl.BlockSpec((rows, chunk), lambda k: (0, k))] * 2,
        scratch_shapes=[pltpu.VMEM((2, 2, rows, 2 * HDIM), BF16)],
        compiler_params=params(),
        name="grad_norm",
    )(info, gq.reshape(2, 2, rows, REP * HDIM), dkv, halo_back, static_back, ddyn, q_weight, kv_weight, q_weight, kv_weight)
    grad_norm = finish(keep, send)

    u = hidden.astype(F32)
    inv_rms = lax.rsqrt(jnp.mean(u * u, axis=1, keepdims=True) + EPS)
    scaled = u * inv_rms
    grad_in = inv_rms * (grad_norm - scaled * jnp.mean(grad_norm * scaled, axis=1, keepdims=True))
    return (combined, grad_in.astype(BF16))


def split(count):
    inner = 1
    while (2 * inner) ** 2 <= count:
        inner *= 2
    return count // inner, inner


def solution(mesh):
    na, nb = split(mesh.shape["ctx"] // 2)
    grid = Mesh(mesh.devices.reshape(mesh.shape["groups"], na, nb, 2), ("x", "a", "b", "c"))
    return jax.shard_map(
        body,
        mesh=grid,
        in_specs=(
            P(("x", "a", "b", "c"), None),
            P(("a", "b", "c"), None),
            P(("a", "b", "c"), None),
            P(("a", "b", "c"), None),
            P("x"),
            P(("x", "a", "b", "c"), None),
        ),
        out_specs=(P(("x", "a", "b", "c"), None), P(("x", "a", "b", "c"), None)),
        check_vma=False,
    )
```

```python
import jax
import jax.numpy as jnp
from jax import lax
from jax.experimental import pallas as pl
from jax.experimental.pallas import tpu as pltpu
from jax.sharding import Mesh, PartitionSpec as P

HEADS = 16
KVH = 4
HDIM = 128
BLK = 128
REP = HEADS // KVH
EPS = 1e-05
SCALE = HDIM ** (-0.5)
F32 = jnp.float32
BF16 = jnp.bfloat16
VMEM = 56 * 1024 * 1024


def dot(a, b, ca, cb):
    return lax.dot_general(a, b, (((ca,), (cb,)), ((), ())), preferred_element_type=F32)


def flip_matrix(n):
    i = lax.broadcasted_iota(jnp.int32, (n, n), 0)
    j = lax.broadcasted_iota(jnp.int32, (n, n), 1)
    return jnp.where(i + j == n - 1, 1.0, 0.0).astype(BF16)


def params():
    return pltpu.CompilerParams(vmem_limit_bytes=VMEM)


def whole():
    return pl.BlockSpec(memory_space=pltpu.VMEM)


def smem():
    return pl.BlockSpec(memory_space=pltpu.SMEM)


def norm_kernel(h00, h01, h10, h11, out):
    core = lax.axis_index("c")
    flip = flip_matrix(128)
    for side, refs in enumerate(((h00, h01), (h10, h11))):
        place = core if side == 0 else 1 - core
        for grp in range(2):
            u = refs[grp][...].astype(F32)
            inv = lax.rsqrt(jnp.mean(u * u, axis=1, keepdims=True) + EPS)
            n = (u * inv).astype(BF16)
            row = pl.multiple_of(place * (2 * BLK) + grp * BLK, BLK)
            out[0, pl.ds(row, BLK), :] = n
            count = n.shape[1] // 128
            for k in range(count):
                m = count - 1 - k
                out[1, pl.ds(row, BLK), m * 128 : m * 128 + 128] = dot(
                    n[:, k * 128 : k * 128 + 128], flip, 1, 0
                ).astype(BF16)


def grad_att_kernel(c00, c01, c10, c11, *refs):
    pieces, (out, w) = refs[:8], refs[8:]
    core = lax.axis_index("c")
    own = lax.axis_index("b") % 2
    half = pieces[0].shape[1]
    rows = pieces[0].shape[0]
    for i in range(4):
        row = pl.multiple_of((own if i < 2 else 1 - own) * rows, rows)
        column = (i % 2) * half
        w[pl.ds(row, rows), column : column + half] = pieces[2 * i][...] + pieces[2 * i + 1][...]
    for side, refs in enumerate(((c00, c01), (c10, c11))):
        place = core if side == 0 else 1 - core
        rows = jnp.concatenate([refs[0][...], refs[1][...]], axis=0)
        row = pl.multiple_of(place * (2 * BLK), 2 * BLK)
        out[pl.ds(row, 2 * BLK), :] = dot(rows, w[...], 1, 1).astype(BF16)


def position():
    return lax.axis_index("a") * lax.axis_size("b") + lax.axis_index("b")


def last_block():
    return 2 * lax.axis_size("a") * lax.axis_size("b") - 1


def attention_kernel(chosen, q, ga, kv, near_p, near_m, far_p, far_m, att, gq, dkv, dnear_p, dnear_m, dfar_p, dfar_m):
    last = last_block()
    t = position()
    g_dyn = chosen[pl.program_id(0)]
    for strand in range(2):
        near, far, dnear, dfar = ((near_p, far_p, dnear_p, dfar_p), (near_m, far_m, dnear_m, dfar_m))[strand]
        sets = [kv[strand, 0, 0], kv[strand, 1, 0], near[0], far[0, 0], far[1, 0]]
        stat_block = last if strand == 0 else 0
        dyn_block = g_dyn if strand == 0 else last - g_dyn
        sums = [None] * 5
        for side in range(2):
            block = 2 * t + side
            next_to = block - 1 if strand == 0 else block + 1
            if strand == 0:
                near_set = 2 if side == 0 else 0
            else:
                near_set = 1 if side == 0 else 2
            order = (near_set, side, 3, 4)
            flags = (
                (next_to >= 0) & (next_to <= last),
                None,
                (stat_block != block) & (stat_block != next_to),
                (dyn_block != block) & (dyn_block != next_to),
            )
            keys = jnp.concatenate([sets[i][:, :HDIM] for i in order], axis=0)
            values = jnp.concatenate([sets[i][:, HDIM:] for i in order], axis=0)
            qs = q[strand, side, 0]
            gs = ga[side, 0]
            rows = jnp.concatenate([qs[:, i * HDIM : (i + 1) * HDIM] for i in range(REP)], axis=0)
            ups = jnp.concatenate([gs[:, i * HDIM : (i + 1) * HDIM] for i in range(REP)], axis=0)
            s = dot(rows, keys, 1, 1) * SCALE
            parts = []
            for i in range(4):
                part = s[:, i * BLK : (i + 1) * BLK]
                if flags[i] is not None:
                    part = jnp.where(flags[i], part, -jnp.inf)
                parts.append(part)
            s = jnp.concatenate(parts, axis=1)
            e = jnp.exp(s - jnp.max(s, axis=1, keepdims=True))
            p = e * (1.0 / jnp.sum(e, axis=1, keepdims=True))
            ph = p.astype(BF16)
            o = dot(ph, values, 1, 0)
            dp = dot(ups, values, 1, 1)
            center = jnp.sum(p * dp, axis=1, keepdims=True)
            ds = (p * (dp - center) * SCALE).astype(BF16)
            dq = dot(ds, keys, 1, 0)
            dk = dot(ds, rows, 0, 0)
            dv = dot(ph, ups, 0, 0)
            for i in range(REP):
                att[strand, side, 0, :, i * HDIM : (i + 1) * HDIM] = o[i * BLK : (i + 1) * BLK].astype(BF16)
                gq[strand, side, 0, :, i * HDIM : (i + 1) * HDIM] = dq[i * BLK : (i + 1) * BLK].astype(BF16)
            for i in range(4):
                term = (dk[i * BLK : (i + 1) * BLK], dv[i * BLK : (i + 1) * BLK])
                old = sums[order[i]]
                sums[order[i]] = term if old is None else (old[0] + term[0], old[1] + term[1])
        targets = (dkv.at[strand, 0, 0], dkv.at[strand, 1, 0], dnear.at[0], dfar.at[0, 0], dfar.at[1, 0])
        for target, (dk, dv) in zip(targets, sums):
            target[:, :HDIM] = dk.astype(target.dtype)
            target[:, HDIM:] = dv.astype(target.dtype)


def output_kernel(att, w, keep, send):
    core = lax.axis_index("c")
    for target, place in ((keep, core), (send, 1 - core)):
        total = dot(att[0, place], w[...], 1, 0) + dot(att[1, place], w[...], 1, 0)
        target[...] = total.astype(target.dtype)


def query_part_kernel(gq, w, wm, part, wkv, wkvf):
    core = lax.axis_index("c")
    flipped = dot(flip_matrix(w.shape[0]), wm[...], 1, 0).astype(BF16)
    wkv[...] = w[:, : 2 * HDIM]
    wkvf[...] = flipped[:, : 2 * HDIM]
    for i, place in enumerate((core, 1 - core)):
        part[i] = dot(gq[0, place], w[:, 2 * HDIM :], 1, 1) + dot(gq[1, place], flipped[:, 2 * HDIM :], 1, 1)


def key_part_kernel(chosen, dkv, near_p, near_m, far_p, far_m, part, wkv, wkvf, keep, send, kg):
    core = lax.axis_index("c")
    t = position()
    last = last_block()

    @pl.when(pl.program_id(0) == 0)
    def _():
        for strand in range(2):
            stat_block = last if strand == 0 else 0
            near, far = ((near_p, far_p), (near_m, far_m))[strand]
            for side in range(2):
                for grp in range(2):
                    total = dkv[strand, side, grp]
                    if side != strand:
                        total = total + near[grp].astype(F32)
                        total = total + jnp.where(2 * t + side == stat_block, far[0, grp].astype(F32), 0.0)
                    dyn_block = chosen[grp] if strand == 0 else last - chosen[grp]
                    total = total + jnp.where(2 * t + side == dyn_block, far[1, grp].astype(F32), 0.0)
                    kg[strand, side, grp * BLK : (grp + 1) * BLK, :] = total.astype(BF16)

    for i, (target, place) in enumerate(((keep, core), (send, 1 - core))):
        total = part[i] + dot(kg[0, place], wkv[...], 1, 1) + dot(kg[1, place], wkvf[...], 1, 1)
        target[...] = total.astype(target.dtype)


def head_group(x, c):
    return x + c * (3 - 2 * x)


def cost(flops, moved):
    return pl.CostEstimate(flops=flops, transcendentals=0, bytes_accessed=moved)


def swap(value, axis):
    return lax.ppermute(value, axis, [(0, 1), (1, 0)])


def after(value, *others):
    return lax.optimization_barrier((value,) + others)[0]


def pair(own, other, index):
    return jnp.where(index == 0, jnp.concatenate([own, other], 0), jnp.concatenate([other, own], 0))


def ring(value, axis):
    count = lax.axis_size(axis)
    return lax.ppermute(value, axis, [(i, (i + 1) % count) for i in range(count)])


def gather_rows(chunk, held):
    na, nb = lax.axis_size("a"), lax.axis_size("b")
    a, b = lax.axis_index("a"), lax.axis_index("b")
    size = chunk.shape[0]
    full = jnp.zeros((na * nb * size, chunk.shape[1]), chunk.dtype)
    across = []
    for step in range(na):
        if 0 < step:
            chunk = ring(after(chunk, *held.get(step, ()), *across[: step - 1][-1:]), "a")
        inner = chunk
        for turn in range(nb):
            pos = ((a - step) % na) * nb + (b - turn) % nb
            full = lax.dynamic_update_slice(full, inner, (pos * size, 0))
            if turn + 1 < nb:
                if step + 1 == na and turn == 0:
                    inner = after(inner, *held.get(-1, ()), *across[-1:])
                inner = ring(inner, "b")
        across.append(inner)
    return full, chunk


def output_rows(w_out, x, a, b, c, held, arrived):
    na, nb = lax.axis_size("a"), lax.axis_size("b")
    mine = head_group(x, c)
    half = w_out.shape[1] // 2
    if (na, nb) != (4, 2):
        full = lax.all_gather(w_out, ("a", "b", "c"), axis=0, tiled=True)
        rows = REP * HDIM // 2
        place = b % 2
        pieces = []
        for where in (place, 1 - place):
            piece = lax.dynamic_slice(full, (mine * 2 * rows + where * rows, 0), (rows, full.shape[1]))
            pieces += [piece[:, :half], piece[:, half:]]
        return [(piece, jnp.zeros_like(piece)) for piece in pieces]
    source = pair(w_out, swap(w_out, "c"), c)
    current = jnp.where(a == mine, source, 0).astype(source.dtype)

    def spot(x, a, c):
        return (x * na + a) * 2 + c

    def send(value, moves):
        pairs = []
        for (sx, sc), (i, j) in moves.items():
            pairs.append((spot(sx, i, sc), spot(sx, j, sc)))
        return lax.ppermute(value, ("x", "a", "c"), pairs)

    def across(value, holders):
        pairs = []
        for (sx, sc), spots in holders.items():
            for i in spots:
                at = (sx * na + i) * 4 + sc
                pairs += [(at, at + 2), (at + 2, at)]
        return lax.ppermute(value, ("x", "a", "b", "c"), pairs)

    start = after(current, held)
    parts = [start[:, :half], start[:, half:]]
    first = [send(v, {(0, 0): (0, 1), (0, 1): (3, 2), (1, 0): (1, 0), (1, 1): (2, 3)}) for v in parts]
    parts = [after(v + w, z) for v, w, z in zip(parts, first, arrived)]
    second = [send(v, {(0, 0): (1, 2), (0, 1): (2, 1), (1, 0): (1, 2), (1, 1): (2, 1)}) for v in parts]
    early = [across(v, {(0, 0): (0, 1), (0, 1): (3, 2), (1, 0): (1, 0), (1, 1): (2, 3)}) for v in parts]
    third = [
        send(after(v, w), {(0, 0): (2, 3), (0, 1): (1, 0), (1, 0): (2, 3), (1, 1): (1, 0)})
        for v, w in zip(second, early)
    ]
    late = [v + w for v, w in zip(second, third)]
    beyond = [across(v, {(0, 0): (2, 3), (0, 1): (1, 0), (1, 0): (2, 3), (1, 1): (1, 0)}) for v in late]
    return list(zip(parts, late)) + list(zip(early, beyond))


def rounds():
    for axis, low in (("b", 1), ("a", lax.axis_size("b"))):
        count = lax.axis_size(axis)
        bit = 1
        while bit < count:
            yield axis, bit * low, [(i, i ^ bit) for i in range(count)]
            bit *= 2


def trade(first, second, t, owner, inward, states, held=()):
    for number, (axis, weight, pairs) in enumerate(rounds()):
        if number == 2:
            first = after(first, *held)
        same = (t // weight) % 2 == (owner // weight) % 2
        give = same != inward
        got = lax.ppermute(jnp.where(give, first, second), axis, pairs)
        states.append(got)
        first, second = jnp.where(give, first, first + got), jnp.where(give, second + got, second)
    return first, second


def body(hidden, w_query, w_keyval, w_out, global_blocks, cotangent):
    x, a, b, c = (lax.axis_index(n) for n in ("x", "a", "b", "c"))
    na, nb = lax.axis_size("a"), lax.axis_size("b")
    n = na * nb
    t = a * nb + b
    blocks = 2 * n
    width = hidden.shape[1]
    mine = head_group(x, c)
    theirs = head_group(x, 1 - c)
    line_up = [(i, i + 1) for i in range(n - 1)]
    line_down = [(i + 1, i) for i in range(n - 1)]

    h10 = swap(hidden, "c")
    h01 = swap(hidden, "x")
    h11 = swap(h01, "c")
    g_own = jnp.sum(global_blocks) - (blocks - 1)
    g_other = swap(after(jnp.full((8, 128), g_own, F32), h01), "x")
    chosen = jnp.stack([g_own, g_other[0, 0].astype(jnp.int32)])
    c10 = swap(cotangent, "c")
    c01 = swap(after(cotangent, g_other), "x")
    c11 = swap(c01, "c")

    half = KVH * HDIM

    def kv_columns(j):
        return jnp.concatenate(
            [
                lax.dynamic_slice_in_dim(w_keyval, j * HDIM, HDIM, 1),
                lax.dynamic_slice_in_dim(w_keyval, half + j * HDIM, HDIM, 1),
            ],
            axis=1,
        )

    def q_columns(j):
        return lax.dynamic_slice_in_dim(w_query, j * REP * HDIM, REP * HDIM, 1)

    normed = pl.pallas_call(
        norm_kernel,
        out_shape=jax.ShapeDtypeStruct((2, 4 * BLK, width), BF16),
        in_specs=[whole()] * 4,
        out_specs=whole(),
        cost_estimate=cost(10**9, 6 * 2**20),
        compiler_params=params(),
        name="norm",
    )(hidden, h01, h10, h11)
    def columns(j):
        return jnp.concatenate([kv_columns(j), q_columns(j)], axis=1)

    held = {3: (h01,), -1: (normed, c01)}
    weight, far_chunk = gather_rows(pair(columns(mine), swap(columns(theirs), "c"), c), held)
    q_weight = weight[:, 2 * HDIM :]
    kv_weight = weight[:, : 2 * HDIM]
    normed = normed.reshape(8 * BLK, width)
    kv = dot(normed, kv_weight, 1, 0).astype(BF16).reshape(2, 2, 2, BLK, 2 * HDIM)

    ctx = ("a", "b")
    up = kv[0, 1]
    down = kv[1, 0]
    near_p, near_m = lax.ppermute(up, ctx, line_up), lax.ppermute(down, ctx, line_down)
    owner = jnp.stack([jnp.full((2,), n - 1, jnp.int32), chosen // 2])
    side = jnp.stack([jnp.ones((2,), jnp.int32), chosen % 2])[:, :, None, None]
    owner = owner[:, :, None, None]
    first = jnp.where(owner == t, jnp.where(side == 0, kv[0, 0], kv[0, 1]), 0).astype(BF16)
    second = jnp.where(n - 1 - owner == t, jnp.where(side == 1, kv[1, 0], kv[1, 1]), 0).astype(BF16)
    first = after(first, c01)
    arrived = []
    first, second = trade(first, second, t, owner, False, arrived)
    wo_parts = output_rows(w_out, x, a, b, c, far_chunk, arrived)

    queries = dot(normed, q_weight, 1, 0).astype(BF16).reshape(2, 2, 2, BLK, REP * HDIM)

    grad_att, o_weight = pl.pallas_call(
        grad_att_kernel,
        out_shape=(
            jax.ShapeDtypeStruct((4 * BLK, REP * HDIM), BF16),
            jax.ShapeDtypeStruct((REP * HDIM, width), BF16),
        ),
        in_specs=[whole()] * 12,
        out_specs=[whole()] * 2,
        cost_estimate=cost(10**9, 9 * 2**20),
        compiler_params=params(),
        name="grad_att",
    )(cotangent, c01, c10, c11, *[v for piece in wo_parts for v in piece])
    grad_att = grad_att.reshape(2, 2, BLK, REP * HDIM)

    wide = pl.BlockSpec((2, 2, 1, BLK, REP * HDIM), lambda g: (0, 0, g, 0, 0))
    pairs_spec = pl.BlockSpec((2, 2, 1, BLK, 2 * HDIM), lambda g: (0, 0, g, 0, 0))
    near_spec = pl.BlockSpec((1, BLK, 2 * HDIM), lambda g: (g, 0, 0))
    far_spec = pl.BlockSpec((2, 1, BLK, 2 * HDIM), lambda g: (0, g, 0, 0))
    near_shape = jax.ShapeDtypeStruct((2, BLK, 2 * HDIM), BF16)
    far_shape = jax.ShapeDtypeStruct((2, 2, BLK, 2 * HDIM), BF16)
    extras = [near_spec, near_spec, far_spec, far_spec]
    att, gq, dkv, dnear_p, dnear_m, dfar_p, dfar_m = pl.pallas_call(
        attention_kernel,
        grid=(2,),
        out_shape=(
            jax.ShapeDtypeStruct(queries.shape, BF16),
            jax.ShapeDtypeStruct(queries.shape, BF16),
            jax.ShapeDtypeStruct(kv.shape, F32),
            near_shape,
            near_shape,
            far_shape,
            far_shape,
        ),
        in_specs=[smem(), wide, pl.BlockSpec((2, 1, BLK, REP * HDIM), lambda g: (0, g, 0, 0)), pairs_spec] + extras,
        out_specs=[wide, wide, pairs_spec] + extras,
        cost_estimate=cost(8 * 10**9, 10 * 2**20),
        compiler_params=params(),
        name="attention",
    )(chosen, queries, grad_att, kv, near_p, near_m, first, second)

    near_p, near_m = lax.ppermute(dnear_p, ctx, line_down), lax.ppermute(dnear_m, ctx, line_up)
    rows = 2 * BLK

    def finish(keep, send):
        got = swap(send, "c")
        total = keep + got.astype(F32)
        return total[:BLK] + swap(total[BLK:].astype(BF16), "x").astype(F32), total

    chunk = width // 4
    partial = (jax.ShapeDtypeStruct((rows, width), F32), jax.ShapeDtypeStruct((rows, width), BF16))
    out_parts = pl.pallas_call(
            output_kernel,
            grid=(width // chunk,),
            out_shape=partial,
            in_specs=[
                pl.BlockSpec((2, 2, rows, REP * HDIM), lambda k: (0, 0, 0, 0)),
                pl.BlockSpec((REP * HDIM, chunk), lambda k: (0, k)),
            ],
            out_specs=[pl.BlockSpec((rows, chunk), lambda k: (0, k))] * 2,
            cost_estimate=cost(2 * 10**9, 7 * 2**20),
            compiler_params=params(),
            name="output",
        )(att.reshape(2, 2, rows, REP * HDIM), o_weight)
    arrived = []
    far_p, far_m = trade(dfar_p, dfar_m, t, owner, True, arrived, (out_parts[1],))
    combined, _ = finish(*out_parts)
    combined = combined.astype(BF16)

    chunk = 256
    steps = width // chunk

    def fixed(shape):
        return pl.BlockSpec(shape, lambda k: (0,) * len(shape))

    part, kv_plain, kv_flipped = pl.pallas_call(
        query_part_kernel,
        grid=(steps,),
        out_shape=(
            jax.ShapeDtypeStruct((2, rows, width), F32),
            jax.ShapeDtypeStruct((width, 2 * HDIM), BF16),
            jax.ShapeDtypeStruct((width, 2 * HDIM), BF16),
        ),
        in_specs=[
            fixed((2, 2, rows, REP * HDIM)),
            pl.BlockSpec((chunk, (2 + REP) * HDIM), lambda k: (k, 0)),
            pl.BlockSpec((chunk, (2 + REP) * HDIM), lambda k: (steps - 1 - k, 0)),
        ],
        out_specs=(
            pl.BlockSpec((2, rows, chunk), lambda k: (0, 0, k)),
            pl.BlockSpec((chunk, 2 * HDIM), lambda k: (k, 0)),
            pl.BlockSpec((chunk, 2 * HDIM), lambda k: (k, 0)),
        ),
        cost_estimate=cost(3 * 10**9, 13 * 2**20),
        compiler_params=params(),
        name="query_part",
    )(after(gq, arrived[1]).reshape(2, 2, rows, REP * HDIM), weight, weight)

    far_p = after(far_p, combined)
    chunk = width // 4
    halves = []
    for start in (0, 2):
        half, total = finish(
                *pl.pallas_call(
                    key_part_kernel,
                    grid=(2,),
                    out_shape=(
                        jax.ShapeDtypeStruct((rows, 2 * chunk), F32),
                        jax.ShapeDtypeStruct((rows, 2 * chunk), BF16),
                    ),
                    in_specs=[
                        smem(),
                        fixed(dkv.shape),
                        fixed(near_shape.shape),
                        fixed(near_shape.shape),
                        fixed(far_shape.shape),
                        fixed(far_shape.shape),
                        pl.BlockSpec((2, rows, chunk), lambda k, start=start: (0, 0, k + start)),
                        pl.BlockSpec((chunk, 2 * HDIM), lambda k, start=start: (k + start, 0)),
                        pl.BlockSpec((chunk, 2 * HDIM), lambda k, start=start: (k + start, 0)),
                    ],
                    out_specs=[pl.BlockSpec((rows, chunk), lambda k: (0, k))] * 2,
                    scratch_shapes=[pltpu.VMEM((2, 2, rows, 2 * HDIM), BF16)],
                    cost_estimate=cost(5 * 10**8, 8 * 2**20),
                    compiler_params=params(),
                    name="key_part",
                )(chosen, dkv, near_p, near_m, far_p, far_m, part, kv_plain, kv_flipped)
        )
        halves.append(half)
        far_p = after(far_p, total)
    grad_norm = jnp.concatenate(halves, axis=1)

    u = hidden.astype(F32)
    inv_rms = lax.rsqrt(jnp.mean(u * u, axis=1, keepdims=True) + EPS)
    scaled = u * inv_rms
    grad_in = inv_rms * (grad_norm - scaled * jnp.mean(grad_norm * scaled, axis=1, keepdims=True))
    return (combined, grad_in.astype(BF16))


def split(count):
    inner = 1
    while (2 * inner) ** 2 <= count:
        inner *= 2
    return count // inner, inner


def solution(mesh):
    na, nb = split(mesh.shape["ctx"] // 2)
    grid = Mesh(mesh.devices.reshape(mesh.shape["groups"], na, nb, 2), ("x", "a", "b", "c"))
    return jax.shard_map(
        body,
        mesh=grid,
        in_specs=(
            P(("x", "a", "b", "c"), None),
            P(("a", "b", "c"), None),
            P(("a", "b", "c"), None),
            P(("a", "b", "c"), None),
            P("x"),
            P(("x", "a", "b", "c"), None),
        ),
        out_specs=(P(("x", "a", "b", "c"), None), P(("x", "a", "b", "c"), None)),
        check_vma=False,
    )
```

```python
import jax
import jax.numpy as jnp
from jax import lax
from jax.experimental import pallas as pl
from jax.experimental.pallas import tpu as pltpu
from jax.sharding import Mesh, PartitionSpec as P

HEADS = 16
KVH = 4
HDIM = 128
BLK = 128
REP = HEADS // KVH
EPS = 1e-05
SCALE = HDIM ** (-0.5)
F32 = jnp.float32
BF16 = jnp.bfloat16
VMEM = 56 * 1024 * 1024


def dot(a, b, ca, cb):
    return lax.dot_general(a, b, (((ca,), (cb,)), ((), ())), preferred_element_type=F32)


def flip_matrix(n):
    i = lax.broadcasted_iota(jnp.int32, (n, n), 0)
    j = lax.broadcasted_iota(jnp.int32, (n, n), 1)
    return jnp.where(i + j == n - 1, 1.0, 0.0).astype(BF16)


def params():
    return pltpu.CompilerParams(vmem_limit_bytes=VMEM)


def whole():
    return pl.BlockSpec(memory_space=pltpu.VMEM)


def smem():
    return pl.BlockSpec(memory_space=pltpu.SMEM)


def norm_kernel(h00, h01, h10, h11, out):
    core = lax.axis_index("c")
    flip = flip_matrix(128)
    for side, refs in enumerate(((h00, h01), (h10, h11))):
        place = core if side == 0 else 1 - core
        for grp in range(2):
            u = refs[grp][...].astype(F32)
            inv = lax.rsqrt(jnp.mean(u * u, axis=1, keepdims=True) + EPS)
            n = (u * inv).astype(BF16)
            row = pl.multiple_of(place * (2 * BLK) + grp * BLK, BLK)
            out[0, pl.ds(row, BLK), :] = n
            count = n.shape[1] // 128
            for k in range(count):
                m = count - 1 - k
                out[1, pl.ds(row, BLK), m * 128 : m * 128 + 128] = dot(
                    n[:, k * 128 : k * 128 + 128], flip, 1, 0
                ).astype(BF16)


def grad_att_kernel(c00, c01, c10, c11, *refs):
    pieces, (out, w) = refs[:8], refs[8:]
    core = lax.axis_index("c")
    own = lax.axis_index("b") % 2
    half = pieces[0].shape[1]
    rows = pieces[0].shape[0]
    for i in range(4):
        row = pl.multiple_of((own if i < 2 else 1 - own) * rows, rows)
        column = (i % 2) * half
        w[pl.ds(row, rows), column : column + half] = pieces[2 * i][...] + pieces[2 * i + 1][...]
    for side, refs in enumerate(((c00, c01), (c10, c11))):
        place = core if side == 0 else 1 - core
        rows = jnp.concatenate([refs[0][...], refs[1][...]], axis=0)
        row = pl.multiple_of(place * (2 * BLK), 2 * BLK)
        out[pl.ds(row, 2 * BLK), :] = dot(rows, w[...], 1, 1).astype(BF16)


def position():
    return lax.axis_index("a") * lax.axis_size("b") + lax.axis_index("b")


def last_block():
    return 2 * lax.axis_size("a") * lax.axis_size("b") - 1


def attention_kernel(chosen, q, ga, kv, near_p, near_m, far_p, far_m, att, gq, dkv, dnear_p, dnear_m, dfar_p, dfar_m, pack):
    last = last_block()
    t = position()
    g_dyn = chosen[pl.program_id(0)]
    for strand in range(2):
        near, far, dnear, dfar = ((near_p, far_p, dnear_p, dfar_p), (near_m, far_m, dnear_m, dfar_m))[strand]
        sets = [kv[strand, 0, 0], kv[strand, 1, 0], near[0], far[0, 0], far[1, 0]]
        stat_block = last if strand == 0 else 0
        dyn_block = g_dyn if strand == 0 else last - g_dyn
        sums = [None] * 5
        for side in range(2):
            block = 2 * t + side
            next_to = block - 1 if strand == 0 else block + 1
            if strand == 0:
                near_set = 2 if side == 0 else 0
            else:
                near_set = 1 if side == 0 else 2
            order = (near_set, side, 3, 4)
            flags = (
                (next_to >= 0) & (next_to <= last),
                None,
                (stat_block != block) & (stat_block != next_to),
                (dyn_block != block) & (dyn_block != next_to),
            )
            keys = jnp.concatenate([sets[i][:, :HDIM] for i in order], axis=0)
            values = jnp.concatenate([sets[i][:, HDIM:] for i in order], axis=0)
            qs = q[strand, side, 0]
            gs = ga[side, 0]
            rows = jnp.concatenate([qs[:, i * HDIM : (i + 1) * HDIM] for i in range(REP)], axis=0)
            ups = jnp.concatenate([gs[:, i * HDIM : (i + 1) * HDIM] for i in range(REP)], axis=0)
            s = dot(rows, keys, 1, 1) * SCALE
            parts = []
            for i in range(4):
                part = s[:, i * BLK : (i + 1) * BLK]
                if flags[i] is not None:
                    part = jnp.where(flags[i], part, -jnp.inf)
                parts.append(part)
            s = jnp.concatenate(parts, axis=1)
            e = jnp.exp(s - jnp.max(s, axis=1, keepdims=True))
            p = e * (1.0 / jnp.sum(e, axis=1, keepdims=True))
            ph = p.astype(BF16)
            o = dot(ph, values, 1, 0)
            dp = dot(ups, values, 1, 1)
            center = jnp.sum(p * dp, axis=1, keepdims=True)
            ds = (p * (dp - center) * SCALE).astype(BF16)
            dq = dot(ds, keys, 1, 0)
            dk = dot(ds, rows, 0, 0)
            dv = dot(ph, ups, 0, 0)
            for i in range(REP):
                att[strand, side, 0, :, i * HDIM : (i + 1) * HDIM] = o[i * BLK : (i + 1) * BLK].astype(BF16)
                gq[strand, side, 0, :, i * HDIM : (i + 1) * HDIM] = dq[i * BLK : (i + 1) * BLK].astype(BF16)
            for i in range(4):
                term = (dk[i * BLK : (i + 1) * BLK], dv[i * BLK : (i + 1) * BLK])
                old = sums[order[i]]
                sums[order[i]] = term if old is None else (old[0] + term[0], old[1] + term[1])
        targets = (dkv.at[strand, 0, 0], dkv.at[strand, 1, 0], dnear.at[0], dfar.at[0, 0], dfar.at[1, 0])
        for target, (dk, dv) in zip(targets, sums):
            target[:, :HDIM] = dk.astype(target.dtype)
            target[:, HDIM:] = dv.astype(target.dtype)
    for i, owner in enumerate((last // 2, g_dyn // 2)):
        pack[i, 0] = jnp.where(t % 2 == owner % 2, dfar_m[i, 0], dfar_p[i, 0])


def output_kernel(att, w, keep, send):
    core = lax.axis_index("c")
    for target, place in ((keep, core), (send, 1 - core)):
        total = dot(att[0, place], w[...], 1, 0) + dot(att[1, place], w[...], 1, 0)
        target[...] = total.astype(target.dtype)


def query_part_kernel(gq, w, wm, part, wkv, wkvf):
    core = lax.axis_index("c")
    flipped = dot(flip_matrix(w.shape[0]), wm[...], 1, 0).astype(BF16)
    wkv[...] = w[:, : 2 * HDIM]
    wkvf[...] = flipped[:, : 2 * HDIM]
    for i, place in enumerate((core, 1 - core)):
        part[i] = dot(gq[0, place], w[:, 2 * HDIM :], 1, 1) + dot(gq[1, place], flipped[:, 2 * HDIM :], 1, 1)


def key_part_kernel(chosen, dkv, near_p, near_m, far_p, far_m, part, wkv, wkvf, keep, send, kg):
    core = lax.axis_index("c")
    t = position()
    last = last_block()

    @pl.when(pl.program_id(0) == 0)
    def _():
        for strand in range(2):
            stat_block = last if strand == 0 else 0
            near, far = ((near_p, far_p), (near_m, far_m))[strand]
            for side in range(2):
                for grp in range(2):
                    total = dkv[strand, side, grp]
                    if side != strand:
                        total = total + near[grp].astype(F32)
                        total = total + jnp.where(2 * t + side == stat_block, far[0, grp].astype(F32), 0.0)
                    dyn_block = chosen[grp] if strand == 0 else last - chosen[grp]
                    total = total + jnp.where(2 * t + side == dyn_block, far[1, grp].astype(F32), 0.0)
                    kg[strand, side, grp * BLK : (grp + 1) * BLK, :] = total.astype(BF16)

    for i, (target, place) in enumerate(((keep, core), (send, 1 - core))):
        total = part[i] + dot(kg[0, place], wkv[...], 1, 1) + dot(kg[1, place], wkvf[...], 1, 1)
        target[...] = total.astype(target.dtype)


def head_group(x, c):
    return x + c * (3 - 2 * x)


def cost(flops, moved):
    return pl.CostEstimate(flops=flops, transcendentals=0, bytes_accessed=moved)


def swap(value, axis):
    return lax.ppermute(value, axis, [(0, 1), (1, 0)])


def after(value, *others):
    return lax.optimization_barrier((value,) + others)[0]


def pair(own, other, index):
    return jnp.where(index == 0, jnp.concatenate([own, other], 0), jnp.concatenate([other, own], 0))


def ring(value, axis):
    count = lax.axis_size(axis)
    return lax.ppermute(value, axis, [(i, (i + 1) % count) for i in range(count)])


def gather_rows(chunk, held):
    na, nb = lax.axis_size("a"), lax.axis_size("b")
    a, b = lax.axis_index("a"), lax.axis_index("b")
    size = chunk.shape[0]
    full = jnp.zeros((na * nb * size, chunk.shape[1]), chunk.dtype)
    across = []
    for step in range(na):
        if 0 < step:
            chunk = ring(after(chunk, *held.get(step, ()), *across[: step - 1][-1:]), "a")
        inner = chunk
        for turn in range(nb):
            pos = ((a - step) % na) * nb + (b - turn) % nb
            full = lax.dynamic_update_slice(full, inner, (pos * size, 0))
            if turn + 1 < nb:
                if step + 1 == na and turn == 0:
                    inner = after(inner, *held.get(-1, ()), *across[-1:])
                inner = ring(inner, "b")
        across.append(inner)
    return full, chunk


def output_rows(w_out, x, a, b, c, held, arrived, kv):
    na, nb = lax.axis_size("a"), lax.axis_size("b")
    mine = head_group(x, c)
    half = w_out.shape[1] // 2
    if (na, nb) != (4, 2):
        full = lax.all_gather(w_out, ("a", "b", "c"), axis=0, tiled=True)
        rows = REP * HDIM // 2
        place = b % 2
        pieces = []
        for where in (place, 1 - place):
            piece = lax.dynamic_slice(full, (mine * 2 * rows + where * rows, 0), (rows, full.shape[1]))
            pieces += [piece[:, :half], piece[:, half:]]
        return [(piece, jnp.zeros_like(piece)) for piece in pieces]
    source = pair(w_out, swap(w_out, "c"), c)
    current = jnp.where(a == mine, source, 0).astype(source.dtype)

    def spot(x, a, c):
        return (x * na + a) * 2 + c

    def send(value, moves):
        pairs = []
        for (sx, sc), (i, j) in moves.items():
            pairs.append((spot(sx, i, sc), spot(sx, j, sc)))
        return lax.ppermute(value, ("x", "a", "c"), pairs)

    def across(value, holders):
        pairs = []
        for (sx, sc), spots in holders.items():
            for i in spots:
                at = (sx * na + i) * 4 + sc
                pairs += [(at, at + 2), (at + 2, at)]
        return lax.ppermute(value, ("x", "a", "b", "c"), pairs)

    start = after(current, held)
    parts = [start[:, :half], start[:, half:]]
    first = [send(v, {(0, 0): (0, 1), (0, 1): (3, 2), (1, 0): (1, 0), (1, 1): (2, 3)}) for v in parts]
    parts = [after(parts[0] + first[0], kv), after(parts[1] + first[1], arrived[0])]
    second = [send(v, {(0, 0): (1, 2), (0, 1): (2, 1), (1, 0): (1, 2), (1, 1): (2, 1)}) for v in parts]
    early = [across(v, {(0, 0): (0, 1), (0, 1): (3, 2), (1, 0): (1, 0), (1, 1): (2, 3)}) for v in parts]
    third = [
        send(after(v, w), {(0, 0): (2, 3), (0, 1): (1, 0), (1, 0): (2, 3), (1, 1): (1, 0)})
        for v, w in zip(second, early)
    ]
    late = [v + w for v, w in zip(second, third)]
    beyond = [across(v, {(0, 0): (2, 3), (0, 1): (1, 0), (1, 0): (2, 3), (1, 1): (1, 0)}) for v in late]
    return list(zip(parts, late)) + list(zip(early, beyond))


def rounds():
    for axis, low in (("b", 1), ("a", lax.axis_size("b"))):
        count = lax.axis_size(axis)
        bit = 1
        while bit < count:
            yield axis, bit * low, [(i, i ^ bit) for i in range(count)]
            bit *= 2


def trade(first, second, t, owner, inward, states, held=(), packed=None):
    for number, (axis, weight, pairs) in enumerate(rounds()):
        if number == 2:
            first = after(first, *held)
        same = (t // weight) % 2 == (owner // weight) % 2
        give = same != inward
        if number > 0 or packed is None:
            packed = jnp.where(give, first, second)
        got = lax.ppermute(packed, axis, pairs)
        states.append(got)
        first, second = jnp.where(give, first, first + got), jnp.where(give, second + got, second)
    return first, second


def body(hidden, w_query, w_keyval, w_out, global_blocks, cotangent):
    x, a, b, c = (lax.axis_index(n) for n in ("x", "a", "b", "c"))
    na, nb = lax.axis_size("a"), lax.axis_size("b")
    n = na * nb
    t = a * nb + b
    blocks = 2 * n
    width = hidden.shape[1]
    mine = head_group(x, c)
    theirs = head_group(x, 1 - c)
    line_up = [(i, i + 1) for i in range(n - 1)]
    line_down = [(i + 1, i) for i in range(n - 1)]

    h10 = swap(hidden, "c")
    h01 = swap(hidden, "x")
    h11 = swap(h01, "c")
    g_own = jnp.sum(global_blocks) - (blocks - 1)
    g_other = swap(after(jnp.full((8, 128), g_own, F32), h01), "x")
    chosen = jnp.stack([g_own, g_other[0, 0].astype(jnp.int32)])
    c10 = swap(cotangent, "c")
    c01 = swap(after(cotangent, g_other), "x")
    c11 = swap(c01, "c")

    half = KVH * HDIM

    def kv_columns(j):
        return jnp.concatenate(
            [
                lax.dynamic_slice_in_dim(w_keyval, j * HDIM, HDIM, 1),
                lax.dynamic_slice_in_dim(w_keyval, half + j * HDIM, HDIM, 1),
            ],
            axis=1,
        )

    def q_columns(j):
        return lax.dynamic_slice_in_dim(w_query, j * REP * HDIM, REP * HDIM, 1)

    normed = pl.pallas_call(
        norm_kernel,
        out_shape=jax.ShapeDtypeStruct((2, 4 * BLK, width), BF16),
        in_specs=[whole()] * 4,
        out_specs=whole(),
        cost_estimate=cost(10**9, 6 * 2**20),
        compiler_params=params(),
        name="norm",
    )(hidden, h01, h10, h11)
    def columns(j):
        return jnp.concatenate([kv_columns(j), q_columns(j)], axis=1)

    held = {3: (h01,), -1: (normed, c01)}
    weight, far_chunk = gather_rows(pair(columns(mine), swap(columns(theirs), "c"), c), held)
    q_weight = weight[:, 2 * HDIM :]
    kv_weight = weight[:, : 2 * HDIM]
    normed = normed.reshape(8 * BLK, width)
    kv = dot(normed, kv_weight, 1, 0).astype(BF16).reshape(2, 2, 2, BLK, 2 * HDIM)

    ctx = ("a", "b")
    up = kv[0, 1]
    down = kv[1, 0]
    near_p, near_m = lax.ppermute(up, ctx, line_up), lax.ppermute(down, ctx, line_down)
    owner = jnp.stack([jnp.full((2,), n - 1, jnp.int32), chosen // 2])
    side = jnp.stack([jnp.ones((2,), jnp.int32), chosen % 2])[:, :, None, None]
    owner = owner[:, :, None, None]
    first = jnp.where(owner == t, jnp.where(side == 0, kv[0, 0], kv[0, 1]), 0).astype(BF16)
    second = jnp.where(n - 1 - owner == t, jnp.where(side == 1, kv[1, 0], kv[1, 1]), 0).astype(BF16)
    first = after(first, c01)
    arrived = []
    first, second = trade(first, second, t, owner, False, arrived)
    wo_parts = output_rows(w_out, x, a, b, c, far_chunk, arrived, kv)

    queries = dot(normed, q_weight, 1, 0).astype(BF16).reshape(2, 2, 2, BLK, REP * HDIM)

    grad_att, o_weight = pl.pallas_call(
        grad_att_kernel,
        out_shape=(
            jax.ShapeDtypeStruct((4 * BLK, REP * HDIM), BF16),
            jax.ShapeDtypeStruct((REP * HDIM, width), BF16),
        ),
        in_specs=[whole()] * 12,
        out_specs=[whole()] * 2,
        cost_estimate=cost(10**9, 9 * 2**20),
        compiler_params=params(),
        name="grad_att",
    )(cotangent, c01, c10, c11, *[v for piece in wo_parts for v in piece])
    grad_att = grad_att.reshape(2, 2, BLK, REP * HDIM)

    wide = pl.BlockSpec((2, 2, 1, BLK, REP * HDIM), lambda g: (0, 0, g, 0, 0))
    pairs_spec = pl.BlockSpec((2, 2, 1, BLK, 2 * HDIM), lambda g: (0, 0, g, 0, 0))
    near_spec = pl.BlockSpec((1, BLK, 2 * HDIM), lambda g: (g, 0, 0))
    far_spec = pl.BlockSpec((2, 1, BLK, 2 * HDIM), lambda g: (0, g, 0, 0))
    near_shape = jax.ShapeDtypeStruct((2, BLK, 2 * HDIM), BF16)
    far_shape = jax.ShapeDtypeStruct((2, 2, BLK, 2 * HDIM), BF16)
    extras = [near_spec, near_spec, far_spec, far_spec]
    att, gq, dkv, dnear_p, dnear_m, dfar_p, dfar_m, pack = pl.pallas_call(
        attention_kernel,
        grid=(2,),
        out_shape=(
            jax.ShapeDtypeStruct(queries.shape, BF16),
            jax.ShapeDtypeStruct(queries.shape, BF16),
            jax.ShapeDtypeStruct(kv.shape, F32),
            near_shape,
            near_shape,
            far_shape,
            far_shape,
            far_shape,
        ),
        in_specs=[smem(), wide, pl.BlockSpec((2, 1, BLK, REP * HDIM), lambda g: (0, g, 0, 0)), pairs_spec] + extras,
        out_specs=[wide, wide, pairs_spec] + extras + [far_spec],
        cost_estimate=cost(8 * 10**9, 10 * 2**20),
        compiler_params=params(),
        name="attention",
    )(chosen, queries, grad_att, kv, near_p, near_m, first, second)

    near_p, near_m = lax.ppermute(dnear_p, ctx, line_down), lax.ppermute(dnear_m, ctx, line_up)
    rows = 2 * BLK

    def finish(keep, send):
        total = keep + swap(send, "c").astype(F32)
        return total[:BLK] + swap(total[BLK:].astype(BF16), "x").astype(F32), total

    chunk = width // 4
    partial = (jax.ShapeDtypeStruct((rows, width), F32), jax.ShapeDtypeStruct((rows, width), BF16))
    out_parts = pl.pallas_call(
            output_kernel,
            grid=(width // chunk,),
            out_shape=partial,
            in_specs=[
                pl.BlockSpec((2, 2, rows, REP * HDIM), lambda k: (0, 0, 0, 0)),
                pl.BlockSpec((REP * HDIM, chunk), lambda k: (0, k)),
            ],
            out_specs=[pl.BlockSpec((rows, chunk), lambda k: (0, k))] * 2,
            cost_estimate=cost(2 * 10**9, 7 * 2**20),
            compiler_params=params(),
            name="output",
        )(att.reshape(2, 2, rows, REP * HDIM), o_weight)
    arrived = []
    far_p, far_m = trade(dfar_p, dfar_m, t, owner, True, arrived, (out_parts[1],), pack)
    combined, _ = finish(*out_parts)
    combined = combined.astype(BF16)

    chunk = 256
    steps = width // chunk

    def fixed(shape):
        return pl.BlockSpec(shape, lambda k: (0,) * len(shape))

    part, kv_plain, kv_flipped = pl.pallas_call(
        query_part_kernel,
        grid=(steps,),
        out_shape=(
            jax.ShapeDtypeStruct((2, rows, width), F32),
            jax.ShapeDtypeStruct((width, 2 * HDIM), BF16),
            jax.ShapeDtypeStruct((width, 2 * HDIM), BF16),
        ),
        in_specs=[
            fixed((2, 2, rows, REP * HDIM)),
            pl.BlockSpec((chunk, (2 + REP) * HDIM), lambda k: (k, 0)),
            pl.BlockSpec((chunk, (2 + REP) * HDIM), lambda k: (steps - 1 - k, 0)),
        ],
        out_specs=(
            pl.BlockSpec((2, rows, chunk), lambda k: (0, 0, k)),
            pl.BlockSpec((chunk, 2 * HDIM), lambda k: (k, 0)),
            pl.BlockSpec((chunk, 2 * HDIM), lambda k: (k, 0)),
        ),
        cost_estimate=cost(3 * 10**9, 13 * 2**20),
        compiler_params=params(),
        name="query_part",
    )(after(gq, arrived[1]).reshape(2, 2, rows, REP * HDIM), weight, weight)

    far_p = after(far_p, combined)
    chunk = width // 4
    halves = []
    for start in (0, 2):
        half, total = finish(
                *pl.pallas_call(
                    key_part_kernel,
                    grid=(2,),
                    out_shape=(
                        jax.ShapeDtypeStruct((rows, 2 * chunk), F32),
                        jax.ShapeDtypeStruct((rows, 2 * chunk), BF16),
                    ),
                    in_specs=[
                        smem(),
                        fixed(dkv.shape),
                        fixed(near_shape.shape),
                        fixed(near_shape.shape),
                        fixed(far_shape.shape),
                        fixed(far_shape.shape),
                        pl.BlockSpec((2, rows, chunk), lambda k, start=start: (0, 0, k + start)),
                        pl.BlockSpec((chunk, 2 * HDIM), lambda k, start=start: (k + start, 0)),
                        pl.BlockSpec((chunk, 2 * HDIM), lambda k, start=start: (k + start, 0)),
                    ],
                    out_specs=[pl.BlockSpec((rows, chunk), lambda k: (0, k))] * 2,
                    scratch_shapes=[pltpu.VMEM((2, 2, rows, 2 * HDIM), BF16)],
                    cost_estimate=cost(5 * 10**8, 8 * 2**20),
                    compiler_params=params(),
                    name="key_part",
                )(chosen, dkv, near_p, near_m, far_p, far_m, part, kv_plain, kv_flipped)
        )
        halves.append(half)
        far_p = after(far_p, total)
    grad_norm = jnp.concatenate(halves, axis=1)

    u = hidden.astype(F32)
    inv_rms = lax.rsqrt(jnp.mean(u * u, axis=1, keepdims=True) + EPS)
    scaled = u * inv_rms
    grad_in = inv_rms * (grad_norm - scaled * jnp.mean(grad_norm * scaled, axis=1, keepdims=True))
    return (combined, grad_in.astype(BF16))


def split(count):
    inner = 1
    while (2 * inner) ** 2 <= count:
        inner *= 2
    return count // inner, inner


def solution(mesh):
    na, nb = split(mesh.shape["ctx"] // 2)
    grid = Mesh(mesh.devices.reshape(mesh.shape["groups"], na, nb, 2), ("x", "a", "b", "c"))
    return jax.shard_map(
        body,
        mesh=grid,
        in_specs=(
            P(("x", "a", "b", "c"), None),
            P(("a", "b", "c"), None),
            P(("a", "b", "c"), None),
            P(("a", "b", "c"), None),
            P("x"),
            P(("x", "a", "b", "c"), None),
        ),
        out_specs=(P(("x", "a", "b", "c"), None), P(("x", "a", "b", "c"), None)),
        check_vma=False,
    )
```

```python
import jax
import jax.numpy as jnp
from jax import lax
from jax.experimental import pallas as pl
from jax.experimental.pallas import tpu as pltpu
from jax.sharding import Mesh, PartitionSpec as P

HEADS = 16
KVH = 4
HDIM = 128
BLK = 128
REP = HEADS // KVH
EPS = 1e-05
SCALE = HDIM ** (-0.5)
LOG2E = 1.4426950408889634
F32 = jnp.float32
BF16 = jnp.bfloat16
VMEM = 56 * 1024 * 1024


def dot(a, b, ca, cb):
    return lax.dot_general(a, b, (((ca,), (cb,)), ((), ())), preferred_element_type=F32)


def flip_matrix(n):
    i = lax.broadcasted_iota(jnp.int32, (n, n), 0)
    j = lax.broadcasted_iota(jnp.int32, (n, n), 1)
    return jnp.where(i + j == n - 1, 1.0, 0.0).astype(BF16)


def params():
    return pltpu.CompilerParams(vmem_limit_bytes=VMEM)


def whole():
    return pl.BlockSpec(memory_space=pltpu.VMEM)


def smem():
    return pl.BlockSpec(memory_space=pltpu.SMEM)


def norm_kernel(h00, h01, h10, h11, out):
    core = lax.axis_index("c")
    flip = flip_matrix(128)
    for side, refs in enumerate(((h00, h01), (h10, h11))):
        place = core if side == 0 else 1 - core
        for grp in range(2):
            u = refs[grp][...].astype(F32)
            inv = lax.rsqrt(jnp.mean(u * u, axis=1, keepdims=True) + EPS)
            n = (u * inv).astype(BF16)
            row = pl.multiple_of(place * (2 * BLK) + grp * BLK, BLK)
            out[0, pl.ds(row, BLK), :] = n
            count = n.shape[1] // 128
            for k in range(count):
                m = count - 1 - k
                out[1, pl.ds(row, BLK), m * 128 : m * 128 + 128] = dot(
                    n[:, k * 128 : k * 128 + 128], flip, 1, 0
                ).astype(BF16)


def grad_att_kernel(c00, c01, c10, c11, *refs):
    pieces, (out, w) = refs[:8], refs[8:]
    core = lax.axis_index("c")
    own = lax.axis_index("b") % 2
    half = pieces[0].shape[1]
    rows = pieces[0].shape[0]
    for i in range(4):
        row = pl.multiple_of((own if i < 2 else 1 - own) * rows, rows)
        column = (i % 2) * half
        w[pl.ds(row, rows), column : column + half] = pieces[2 * i][...] + pieces[2 * i + 1][...]
    for side, refs in enumerate(((c00, c01), (c10, c11))):
        place = core if side == 0 else 1 - core
        rows = jnp.concatenate([refs[0][...], refs[1][...]], axis=0)
        row = pl.multiple_of(place * (2 * BLK), 2 * BLK)
        out[pl.ds(row, 2 * BLK), :] = dot(rows, w[...], 1, 1).astype(BF16)


def position():
    return lax.axis_index("a") * lax.axis_size("b") + lax.axis_index("b")


def last_block():
    return 2 * lax.axis_size("a") * lax.axis_size("b") - 1


def attention_kernel(chosen, q, ga, kv, near_p, near_m, far_p, far_m, att, gq, dkv, dnear_p, dnear_m, dfar_p, dfar_m, pack):
    last = last_block()
    t = position()
    g_dyn = chosen[pl.program_id(0)]
    sums = {}

    def load(strand, side):
        near, far = ((near_p, far_p), (near_m, far_m))[strand]
        sets = [kv.at[strand, 0, 0], kv.at[strand, 1, 0], near.at[0], far.at[0, 0], far.at[1, 0]]
        if strand == 0:
            near_set = 2 if side == 0 else 0
        else:
            near_set = 1 if side == 0 else 2
        order = (near_set, side, 3, 4)
        keys = jnp.concatenate([sets[i][:, :HDIM] for i in order], axis=0)
        values = jnp.concatenate([sets[i][:, HDIM:] for i in order], axis=0)
        rows = jnp.concatenate([q[strand, side, 0, :, i * HDIM : (i + 1) * HDIM] for i in range(REP)], axis=0)
        ups = jnp.concatenate([ga[side, 0, :, i * HDIM : (i + 1) * HDIM] for i in range(REP)], axis=0)
        return order, keys, values, rows, ups, dot(rows, keys, 1, 1), dot(ups, values, 1, 1)

    def weigh(strand, side, s, dp):
        block = 2 * t + side
        stat_block = last if strand == 0 else 0
        dyn_block = g_dyn if strand == 0 else last - g_dyn
        next_to = block - 1 if strand == 0 else block + 1
        flags = (
            (next_to >= 0) & (next_to <= last),
            None,
            (stat_block != block) & (stat_block != next_to),
            (dyn_block != block) & (dyn_block != next_to),
        )
        parts = []
        for i in range(4):
            part = s[:, i * BLK : (i + 1) * BLK]
            parts.append(part if flags[i] is None else jnp.where(flags[i], part, -jnp.inf))
        s = jnp.concatenate(parts, axis=1)
        e = jnp.exp2((s - jnp.max(s, axis=1, keepdims=True)) * (SCALE * LOG2E))
        inverse = 1.0 / jnp.sum(e, axis=1, keepdims=True)
        center = jnp.sum(e * dp, axis=1, keepdims=True) * inverse
        p = e * inverse
        return p.astype(BF16), (p * (dp - center)).astype(BF16)

    def emit(strand, side, order, keys, values, rows, ups, ph, ds):
        o = dot(ph, values, 1, 0).astype(BF16)
        dq = (dot(ds, keys, 1, 0) * SCALE).astype(BF16)
        dk = dot(ds, rows, 0, 0) * SCALE
        dv = dot(ph, ups, 0, 0)
        for i in range(REP):
            att[strand, side, 0, :, i * HDIM : (i + 1) * HDIM] = o[i * BLK : (i + 1) * BLK]
            gq[strand, side, 0, :, i * HDIM : (i + 1) * HDIM] = dq[i * BLK : (i + 1) * BLK]
        for i in range(4):
            term = (dk[i * BLK : (i + 1) * BLK], dv[i * BLK : (i + 1) * BLK])
            old = sums.get((strand, order[i]))
            sums[strand, order[i]] = term if old is None else (old[0] + term[0], old[1] + term[1])
        if side == 1:
            dnear, dfar = ((dnear_p, dfar_p), (dnear_m, dfar_m))[strand]
            targets = (dkv.at[strand, 0, 0], dkv.at[strand, 1, 0], dnear.at[0], dfar.at[0, 0], dfar.at[1, 0])
            for i, target in enumerate(targets):
                target[:, :HDIM] = sums[strand, i][0].astype(target.dtype)
                target[:, HDIM:] = sums[strand, i][1].astype(target.dtype)

    units = [(strand, side) for strand in range(2) for side in range(2)]
    following = load(*units[0])
    ready = None
    for number, unit in enumerate(units):
        *held, s, dp = following
        if number + 1 < len(units):
            following = load(*units[number + 1])
        weighed = weigh(*unit, s, dp)
        if ready is not None:
            emit(*ready)
        ready = (*unit, *held, *weighed)
    emit(*ready)

    for i, owner in enumerate((last // 2, g_dyn // 2)):
        pack[i, 0] = jnp.where(t % 2 == owner % 2, dfar_m[i, 0], dfar_p[i, 0])


def output_kernel(att, w, keep, send):
    core = lax.axis_index("c")
    for target, place in ((keep, core), (send, 1 - core)):
        total = dot(att[0, place], w[...], 1, 0) + dot(att[1, place], w[...], 1, 0)
        target[...] = total.astype(target.dtype)


def query_part_kernel(gq, w, wm, part, wkv, wkvf):
    core = lax.axis_index("c")
    flipped = dot(flip_matrix(w.shape[0]), wm[...], 1, 0).astype(BF16)
    wkv[...] = w[:, : 2 * HDIM]
    wkvf[...] = flipped[:, : 2 * HDIM]
    for i, place in enumerate((core, 1 - core)):
        part[i] = dot(gq[0, place], w[:, 2 * HDIM :], 1, 1) + dot(gq[1, place], flipped[:, 2 * HDIM :], 1, 1)


def project_keys(kg, part, wkv, wkvf, keep, send):
    core = lax.axis_index("c")
    for i, (target, place) in enumerate(((keep, core), (send, 1 - core))):
        total = part[i] + dot(kg[0, place], wkv[...], 1, 1) + dot(kg[1, place], wkvf[...], 1, 1)
        target[...] = total.astype(target.dtype)


def first_key_kernel(chosen, dkv, near_p, near_m, far_p, far_m, part, wkv, wkvf, keep, send, kg):
    t = position()
    last = last_block()

    @pl.when(pl.program_id(0) == 0)
    def _():
        for strand in range(2):
            stat_block = last if strand == 0 else 0
            near, far = ((near_p, far_p), (near_m, far_m))[strand]
            for side in range(2):
                for grp in range(2):
                    total = dkv[strand, side, grp]
                    if side != strand:
                        total = total + near[grp].astype(F32)
                        term = far[0, grp].astype(F32)
                        total = total + jnp.where(2 * t + side == stat_block, term, 0.0)
                    dyn_block = chosen[grp] if strand == 0 else last - chosen[grp]
                    term = far[1, grp].astype(F32)
                    total = total + jnp.where(2 * t + side == dyn_block, term, 0.0)
                    kg[strand, side, grp * BLK : (grp + 1) * BLK, :] = total.astype(BF16)

    project_keys(kg, part, wkv, wkvf, keep, send)


def head_group(x, c):
    return x + c * (3 - 2 * x)


def cost(flops, moved):
    return pl.CostEstimate(flops=flops, transcendentals=0, bytes_accessed=moved)


def swap(value, axis):
    return lax.ppermute(value, axis, [(0, 1), (1, 0)])


def after(value, *others):
    return lax.optimization_barrier((value,) + others)[0]


def pair(own, other, index):
    return jnp.where(index == 0, jnp.concatenate([own, other], 0), jnp.concatenate([other, own], 0))


def ring(value, axis):
    count = lax.axis_size(axis)
    return lax.ppermute(value, axis, [(i, (i + 1) % count) for i in range(count)])


def gather_rows(chunk, held):
    na, nb = lax.axis_size("a"), lax.axis_size("b")
    a, b = lax.axis_index("a"), lax.axis_index("b")
    size = chunk.shape[0]
    full = jnp.zeros((na * nb * size, chunk.shape[1]), chunk.dtype)
    across = []
    for step in range(na):
        if 0 < step:
            chunk = ring(after(chunk, *held.get(step, ()), *across[: step - 1][-1:]), "a")
        inner = chunk
        for turn in range(nb):
            pos = ((a - step) % na) * nb + (b - turn) % nb
            full = lax.dynamic_update_slice(full, inner, (pos * size, 0))
            if turn + 1 < nb:
                if step + 1 == na and turn == 0:
                    inner = after(inner, *held.get(-1, ()), *across[-1:])
                inner = ring(inner, "b")
        across.append(inner)
    return full, chunk


def output_rows(w_out, x, a, b, c, held, arrived, kv, awaited):
    na, nb = lax.axis_size("a"), lax.axis_size("b")
    mine = head_group(x, c)
    half = w_out.shape[1] // 2
    if (na, nb) != (4, 2):
        full = lax.all_gather(w_out, ("a", "b", "c"), axis=0, tiled=True)
        rows = REP * HDIM // 2
        place = b % 2
        pieces = []
        for where in (place, 1 - place):
            piece = lax.dynamic_slice(full, (mine * 2 * rows + where * rows, 0), (rows, full.shape[1]))
            pieces += [piece[:, :half], piece[:, half:]]
        return [(piece, jnp.zeros_like(piece)) for piece in pieces]
    source = pair(w_out, swap(w_out, "c"), c)
    current = jnp.where(a == mine, source, 0).astype(source.dtype)

    def spot(x, a, c):
        return (x * na + a) * 2 + c

    def send(value, moves):
        pairs = []
        for (sx, sc), (i, j) in moves.items():
            pairs.append((spot(sx, i, sc), spot(sx, j, sc)))
        return lax.ppermute(value, ("x", "a", "c"), pairs)

    def across(value, holders):
        pairs = []
        for (sx, sc), spots in holders.items():
            for i in spots:
                at = (sx * na + i) * 4 + sc
                pairs += [(at, at + 2), (at + 2, at)]
        return lax.ppermute(value, ("x", "a", "b", "c"), pairs)

    start = after(current, held)
    parts = [start[:, :half], start[:, half:]]
    first = [send(v, {(0, 0): (0, 1), (0, 1): (3, 2), (1, 0): (1, 0), (1, 1): (2, 3)}) for v in parts]
    parts = [after(parts[0] + first[0], kv), after(parts[1] + first[1], arrived[0])]
    second = [send(v, {(0, 0): (1, 2), (0, 1): (2, 1), (1, 0): (1, 2), (1, 1): (2, 1)}) for v in parts]
    early = [across(v, {(0, 0): (0, 1), (0, 1): (3, 2), (1, 0): (1, 0), (1, 1): (2, 3)}) for v in parts]
    third = [
        send(after(v, w, *awaited), {(0, 0): (2, 3), (0, 1): (1, 0), (1, 0): (2, 3), (1, 1): (1, 0)})
        for v, w in zip(second, early)
    ]
    late = [v + w for v, w in zip(second, third)]
    beyond = [across(v, {(0, 0): (2, 3), (0, 1): (1, 0), (1, 0): (2, 3), (1, 1): (1, 0)}) for v in late]
    return list(zip(parts, late)) + list(zip(early, beyond))


def rounds():
    for axis, low in (("b", 1), ("a", lax.axis_size("b"))):
        count = lax.axis_size(axis)
        bit = 1
        while bit < count:
            yield axis, bit * low, [(i, i ^ bit) for i in range(count)]
            bit *= 2


def trade(first, second, t, owner, inward, states, held=(), packed=None):
    for number, (axis, weight, pairs) in enumerate(rounds()):
        if number == 2:
            first = after(first, *held)
        same = (t // weight) % 2 == (owner // weight) % 2
        give = same != inward
        if number > 0 or packed is None:
            packed = jnp.where(give, first, second)
        got = lax.ppermute(packed, axis, pairs)
        states.append(got)
        first, second = jnp.where(give, first, first + got), jnp.where(give, second + got, second)
    return first, second


def body(hidden, w_query, w_keyval, w_out, global_blocks, cotangent):
    x, a, b, c = (lax.axis_index(n) for n in ("x", "a", "b", "c"))
    na, nb = lax.axis_size("a"), lax.axis_size("b")
    n = na * nb
    t = a * nb + b
    blocks = 2 * n
    width = hidden.shape[1]
    mine = head_group(x, c)
    theirs = head_group(x, 1 - c)
    line_up = [(i, i + 1) for i in range(n - 1)]
    line_down = [(i + 1, i) for i in range(n - 1)]

    h10 = swap(hidden, "c")
    h01 = swap(hidden, "x")
    h11 = swap(h01, "c")
    g_own = jnp.sum(global_blocks) - (blocks - 1)
    g_other = swap(after(jnp.full((8, 128), g_own, F32), h01), "x")
    chosen = jnp.stack([g_own, g_other[0, 0].astype(jnp.int32)])
    c10 = swap(cotangent, "c")
    c01 = swap(after(cotangent, g_other), "x")
    c11 = swap(c01, "c")

    half = KVH * HDIM

    def kv_columns(j):
        return jnp.concatenate(
            [
                lax.dynamic_slice_in_dim(w_keyval, j * HDIM, HDIM, 1),
                lax.dynamic_slice_in_dim(w_keyval, half + j * HDIM, HDIM, 1),
            ],
            axis=1,
        )

    def q_columns(j):
        return lax.dynamic_slice_in_dim(w_query, j * REP * HDIM, REP * HDIM, 1)

    normed = pl.pallas_call(
        norm_kernel,
        out_shape=jax.ShapeDtypeStruct((2, 4 * BLK, width), BF16),
        in_specs=[whole()] * 4,
        out_specs=whole(),
        cost_estimate=cost(10**9, 6 * 2**20),
        compiler_params=params(),
        name="norm",
    )(hidden, h01, h10, h11)
    def columns(j):
        return jnp.concatenate([kv_columns(j), q_columns(j)], axis=1)

    held = {3: (h01,), -1: (normed, c01)}
    weight, far_chunk = gather_rows(pair(columns(mine), swap(columns(theirs), "c"), c), held)
    q_weight = weight[:, 2 * HDIM :]
    kv_weight = weight[:, : 2 * HDIM]
    normed = normed.reshape(8 * BLK, width)
    kv = dot(normed, kv_weight, 1, 0).astype(BF16).reshape(2, 2, 2, BLK, 2 * HDIM)

    ctx = ("a", "b")
    up = kv[0, 1]
    down = kv[1, 0]
    near_p, near_m = lax.ppermute(up, ctx, line_up), lax.ppermute(down, ctx, line_down)
    owner = jnp.stack([jnp.full((2,), n - 1, jnp.int32), chosen // 2])
    side = jnp.stack([jnp.ones((2,), jnp.int32), chosen % 2])[:, :, None, None]
    owner = owner[:, :, None, None]
    first = jnp.where(owner == t, jnp.where(side == 0, kv[0, 0], kv[0, 1]), 0).astype(BF16)
    second = jnp.where(n - 1 - owner == t, jnp.where(side == 1, kv[1, 0], kv[1, 1]), 0).astype(BF16)
    first = after(first, c01)
    arrived = []
    first, second = trade(first, second, t, owner, False, arrived)
    wo_parts = output_rows(w_out, x, a, b, c, far_chunk, arrived, kv, ())

    queries = dot(normed, q_weight, 1, 0).astype(BF16).reshape(2, 2, 2, BLK, REP * HDIM)

    grad_att, o_weight = pl.pallas_call(
        grad_att_kernel,
        out_shape=(
            jax.ShapeDtypeStruct((4 * BLK, REP * HDIM), BF16),
            jax.ShapeDtypeStruct((REP * HDIM, width), BF16),
        ),
        in_specs=[whole()] * 12,
        out_specs=[whole()] * 2,
        cost_estimate=cost(10**9, 9 * 2**20),
        compiler_params=params(),
        name="grad_att",
    )(cotangent, c01, c10, c11, *[v for piece in wo_parts for v in piece])
    grad_att = grad_att.reshape(2, 2, BLK, REP * HDIM)

    wide = pl.BlockSpec((2, 2, 1, BLK, REP * HDIM), lambda g: (0, 0, g, 0, 0))
    pairs_spec = pl.BlockSpec((2, 2, 1, BLK, 2 * HDIM), lambda g: (0, 0, g, 0, 0))
    near_spec = pl.BlockSpec((1, BLK, 2 * HDIM), lambda g: (g, 0, 0))
    far_spec = pl.BlockSpec((2, 1, BLK, 2 * HDIM), lambda g: (0, g, 0, 0))
    near_shape = jax.ShapeDtypeStruct((2, BLK, 2 * HDIM), BF16)
    far_shape = jax.ShapeDtypeStruct((2, 2, BLK, 2 * HDIM), BF16)
    extras = [near_spec, near_spec, far_spec, far_spec]
    att, gq, dkv, dnear_p, dnear_m, dfar_p, dfar_m, pack = pl.pallas_call(
        attention_kernel,
        grid=(2,),
        out_shape=(
            jax.ShapeDtypeStruct(queries.shape, BF16),
            jax.ShapeDtypeStruct(queries.shape, BF16),
            jax.ShapeDtypeStruct(kv.shape, F32),
            near_shape,
            near_shape,
            far_shape,
            far_shape,
            far_shape,
        ),
        in_specs=[smem(), wide, pl.BlockSpec((2, 1, BLK, REP * HDIM), lambda g: (0, g, 0, 0)), pairs_spec] + extras,
        out_specs=[wide, wide, pairs_spec] + extras + [far_spec],
        cost_estimate=cost(8 * 10**9, 10 * 2**20),
        compiler_params=params(),
        name="attention",
    )(chosen, queries, grad_att, kv, near_p, near_m, first, second)

    near_p, near_m = lax.ppermute(dnear_p, ctx, line_down), lax.ppermute(dnear_m, ctx, line_up)
    rows = 2 * BLK

    def finish(keep, send):
        got = swap(send, "c")
        other = (keep[BLK:] + got[BLK:].astype(F32)).astype(BF16)
        back = swap(other, "x")
        return keep[:BLK] + got[:BLK].astype(F32) + back.astype(F32), other, back

    chunk = width // 4
    partial = (jax.ShapeDtypeStruct((rows, width), F32), jax.ShapeDtypeStruct((rows, width), BF16))
    out_parts = pl.pallas_call(
            output_kernel,
            grid=(width // chunk,),
            out_shape=partial,
            in_specs=[
                pl.BlockSpec((2, 2, rows, REP * HDIM), lambda k: (0, 0, 0, 0)),
                pl.BlockSpec((REP * HDIM, chunk), lambda k: (0, k)),
            ],
            out_specs=[pl.BlockSpec((rows, chunk), lambda k: (0, k))] * 2,
            cost_estimate=cost(2 * 10**9, 7 * 2**20),
            compiler_params=params(),
            name="output",
        )(att.reshape(2, 2, rows, REP * HDIM), o_weight)
    arrived = []
    far_p, far_m = trade(dfar_p, dfar_m, t, owner, True, arrived, (out_parts[1],), pack)
    total = out_parts[0] + swap(out_parts[1], "c").astype(F32)
    combined = total[:BLK] + swap(total[BLK:].astype(BF16), "x").astype(F32)
    combined = combined.astype(BF16)

    chunk = 256
    steps = width // chunk

    def fixed(shape):
        return pl.BlockSpec(shape, lambda k: (0,) * len(shape))

    part, kv_plain, kv_flipped = pl.pallas_call(
        query_part_kernel,
        grid=(steps,),
        out_shape=(
            jax.ShapeDtypeStruct((2, rows, width), F32),
            jax.ShapeDtypeStruct((width, 2 * HDIM), BF16),
            jax.ShapeDtypeStruct((width, 2 * HDIM), BF16),
        ),
        in_specs=[
            fixed((2, 2, rows, REP * HDIM)),
            pl.BlockSpec((chunk, (2 + REP) * HDIM), lambda k: (k, 0)),
            pl.BlockSpec((chunk, (2 + REP) * HDIM), lambda k: (steps - 1 - k, 0)),
        ],
        out_specs=(
            pl.BlockSpec((2, rows, chunk), lambda k: (0, 0, k)),
            pl.BlockSpec((chunk, 2 * HDIM), lambda k: (k, 0)),
            pl.BlockSpec((chunk, 2 * HDIM), lambda k: (k, 0)),
        ),
        cost_estimate=cost(3 * 10**9, 13 * 2**20),
        compiler_params=params(),
        name="query_part",
    )(after(gq, arrived[1]).reshape(2, 2, rows, REP * HDIM), weight, weight)

    chunk = width // 4
    halves = (jax.ShapeDtypeStruct((rows, 2 * chunk), F32), jax.ShapeDtypeStruct((rows, 2 * chunk), BF16))
    key_shape = (2, 2, rows, 2 * HDIM)

    def sections(start):
        return [
            pl.BlockSpec((2, rows, chunk), lambda k: (0, 0, k + start)),
            pl.BlockSpec((chunk, 2 * HDIM), lambda k: (k + start, 0)),
            pl.BlockSpec((chunk, 2 * HDIM), lambda k: (k + start, 0)),
        ]

    *first_half, key_grads = pl.pallas_call(
        first_key_kernel,
        grid=(2,),
        out_shape=halves + (jax.ShapeDtypeStruct(key_shape, BF16),),
        in_specs=[smem()]
        + [fixed(v) for v in (dkv.shape, near_shape.shape, near_shape.shape)]
        + [fixed(far_shape.shape)] * 2
        + sections(0),
        out_specs=[pl.BlockSpec((rows, chunk), lambda k: (0, k))] * 2 + [fixed(key_shape)],
        cost_estimate=cost(5 * 10**8, 8 * 2**20),
        compiler_params=params(),
        name="first_key",
    )(chosen, dkv, near_p, near_m, after(far_p, combined), far_m, part, kv_plain, kv_flipped)
    left, other, _ = finish(*first_half)
    right, _, _ = finish(
        *pl.pallas_call(
            project_keys,
            grid=(2,),
            out_shape=halves,
            in_specs=[fixed(key_shape)] + sections(2),
            out_specs=[pl.BlockSpec((rows, chunk), lambda k: (0, k))] * 2,
            cost_estimate=cost(5 * 10**8, 5 * 2**20),
            compiler_params=params(),
            name="second_key",
        )(after(key_grads, other), part, kv_plain, kv_flipped)
    )
    grad_norm = jnp.concatenate([left, right], axis=1)

    u = hidden.astype(F32)
    inv_rms = lax.rsqrt(jnp.mean(u * u, axis=1, keepdims=True) + EPS)
    scaled = u * inv_rms
    grad_in = inv_rms * (grad_norm - scaled * jnp.mean(grad_norm * scaled, axis=1, keepdims=True))
    return (combined, grad_in.astype(BF16))


def split(count):
    inner = 1
    while (2 * inner) ** 2 <= count:
        inner *= 2
    return count // inner, inner


def solution(mesh):
    na, nb = split(mesh.shape["ctx"] // 2)
    grid = Mesh(mesh.devices.reshape(mesh.shape["groups"], na, nb, 2), ("x", "a", "b", "c"))
    return jax.shard_map(
        body,
        mesh=grid,
        in_specs=(
            P(("x", "a", "b", "c"), None),
            P(("a", "b", "c"), None),
            P(("a", "b", "c"), None),
            P(("a", "b", "c"), None),
            P("x"),
            P(("x", "a", "b", "c"), None),
        ),
        out_specs=(P(("x", "a", "b", "c"), None), P(("x", "a", "b", "c"), None)),
        check_vma=False,
    )
```

```python
import jax
import jax.numpy as jnp
from jax import lax
from jax.experimental import pallas as pl
from jax.experimental.pallas import tpu as pltpu
from jax.sharding import Mesh, PartitionSpec as P

HEADS = 16
KVH = 4
HDIM = 128
BLK = 128
REP = HEADS // KVH
EPS = 1e-05
SCALE = HDIM ** (-0.5)
LOG2E = 1.4426950408889634
F32 = jnp.float32
BF16 = jnp.bfloat16
VMEM = 56 * 1024 * 1024


def dot(a, b, ca, cb):
    return lax.dot_general(a, b, (((ca,), (cb,)), ((), ())), preferred_element_type=F32)


def flip_matrix(n):
    i = lax.broadcasted_iota(jnp.int32, (n, n), 0)
    j = lax.broadcasted_iota(jnp.int32, (n, n), 1)
    return jnp.where(i + j == n - 1, 1.0, 0.0).astype(BF16)


def params():
    return pltpu.CompilerParams(vmem_limit_bytes=VMEM)


def whole():
    return pl.BlockSpec(memory_space=pltpu.VMEM)


def smem():
    return pl.BlockSpec(memory_space=pltpu.SMEM)


def norm_kernel(h00, h01, h10, h11, out):
    core = lax.axis_index("c")
    flip = flip_matrix(128)
    for side, refs in enumerate(((h00, h01), (h10, h11))):
        place = core if side == 0 else 1 - core
        for grp in range(2):
            u = refs[grp][...].astype(F32)
            inv = lax.rsqrt(jnp.mean(u * u, axis=1, keepdims=True) + EPS)
            n = (u * inv).astype(BF16)
            row = pl.multiple_of(place * (2 * BLK) + grp * BLK, BLK)
            out[0, pl.ds(row, BLK), :] = n
            count = n.shape[1] // 128
            for k in range(count):
                m = count - 1 - k
                out[1, pl.ds(row, BLK), m * 128 : m * 128 + 128] = dot(
                    n[:, k * 128 : k * 128 + 128], flip, 1, 0
                ).astype(BF16)


def grad_att_kernel(c00, c01, c10, c11, *refs):
    pieces, (out, w) = refs[:8], refs[8:]
    core = lax.axis_index("c")
    own = lax.axis_index("b") % 2
    half = pieces[0].shape[1]
    rows = pieces[0].shape[0]
    for i in range(4):
        row = pl.multiple_of((own if i < 2 else 1 - own) * rows, rows)
        column = (i % 2) * half
        w[pl.ds(row, rows), column : column + half] = pieces[2 * i][...] + pieces[2 * i + 1][...]
    for side, refs in enumerate(((c00, c01), (c10, c11))):
        place = core if side == 0 else 1 - core
        rows = jnp.concatenate([refs[0][...], refs[1][...]], axis=0)
        row = pl.multiple_of(place * (2 * BLK), 2 * BLK)
        out[pl.ds(row, 2 * BLK), :] = dot(rows, w[...], 1, 1).astype(BF16)


def position():
    return lax.axis_index("a") * lax.axis_size("b") + lax.axis_index("b")


def last_block():
    return 2 * lax.axis_size("a") * lax.axis_size("b") - 1


def attention_kernel(chosen, q, ga, kv, near_p, near_m, far_p, far_m, att, gq, dkv, dnear_p, dnear_m, dfar_p, dfar_m, pack):
    last = last_block()
    t = position()
    g_dyn = chosen[pl.program_id(0)]
    sums = {}

    def load(strand, side):
        near, far = ((near_p, far_p), (near_m, far_m))[strand]
        sets = [kv.at[strand, 0, 0], kv.at[strand, 1, 0], near.at[0], far.at[0, 0], far.at[1, 0]]
        if strand == 0:
            near_set = 2 if side == 0 else 0
        else:
            near_set = 1 if side == 0 else 2
        order = (near_set, side, 3, 4)
        keys = jnp.concatenate([sets[i][:, :HDIM] for i in order], axis=0)
        values = jnp.concatenate([sets[i][:, HDIM:] for i in order], axis=0)
        rows = jnp.concatenate([q[strand, side, 0, :, i * HDIM : (i + 1) * HDIM] for i in range(REP)], axis=0)
        ups = jnp.concatenate([ga[side, 0, :, i * HDIM : (i + 1) * HDIM] for i in range(REP)], axis=0)
        return order, keys, values, rows, ups, dot(rows, keys, 1, 1), dot(ups, values, 1, 1)

    def weigh(strand, side, s, dp):
        block = 2 * t + side
        stat_block = last if strand == 0 else 0
        dyn_block = g_dyn if strand == 0 else last - g_dyn
        next_to = block - 1 if strand == 0 else block + 1
        flags = (
            (next_to >= 0) & (next_to <= last),
            None,
            (stat_block != block) & (stat_block != next_to),
            (dyn_block != block) & (dyn_block != next_to),
        )
        parts = []
        for i in range(4):
            part = s[:, i * BLK : (i + 1) * BLK]
            parts.append(part if flags[i] is None else jnp.where(flags[i], part, -jnp.inf))
        s = jnp.concatenate(parts, axis=1)
        e = jnp.exp2((s - jnp.max(s, axis=1, keepdims=True)) * (SCALE * LOG2E))
        inverse = 1.0 / jnp.sum(e, axis=1, keepdims=True)
        center = jnp.sum(e * dp, axis=1, keepdims=True) * inverse
        p = e * inverse
        return p.astype(BF16), (p * (dp - center)).astype(BF16)

    def emit(strand, side, order, keys, values, rows, ups, ph, ds):
        o = dot(ph, values, 1, 0).astype(BF16)
        dq = (dot(ds, keys, 1, 0) * SCALE).astype(BF16)
        dk = dot(ds, rows, 0, 0) * SCALE
        dv = dot(ph, ups, 0, 0)
        for i in range(REP):
            att[strand, side, 0, :, i * HDIM : (i + 1) * HDIM] = o[i * BLK : (i + 1) * BLK]
            gq[strand, side, 0, :, i * HDIM : (i + 1) * HDIM] = dq[i * BLK : (i + 1) * BLK]
        for i in range(4):
            term = (dk[i * BLK : (i + 1) * BLK], dv[i * BLK : (i + 1) * BLK])
            old = sums.get((strand, order[i]))
            sums[strand, order[i]] = term if old is None else (old[0] + term[0], old[1] + term[1])
        if side == 1:
            dnear, dfar = ((dnear_p, dfar_p), (dnear_m, dfar_m))[strand]
            targets = (dkv.at[strand, 0, 0], dkv.at[strand, 1, 0], dnear.at[0], dfar.at[0, 0], dfar.at[1, 0])
            for i, target in enumerate(targets):
                target[:, :HDIM] = sums[strand, i][0].astype(target.dtype)
                target[:, HDIM:] = sums[strand, i][1].astype(target.dtype)

    units = [(strand, side) for strand in range(2) for side in range(2)]
    following = load(*units[0])
    ready = None
    for number, unit in enumerate(units):
        *held, s, dp = following
        if number + 1 < len(units):
            following = load(*units[number + 1])
        weighed = weigh(*unit, s, dp)
        if ready is not None:
            emit(*ready)
        ready = (*unit, *held, *weighed)
    emit(*ready)

    for i, owner in enumerate((last // 2, g_dyn // 2)):
        pack[i, 0] = jnp.where(t % 2 == owner % 2, dfar_m[i, 0], dfar_p[i, 0])


def output_kernel(att, w, keep, send):
    core = lax.axis_index("c")
    for target, place in ((keep, core), (send, 1 - core)):
        total = dot(att[0, place], w[...], 1, 0) + dot(att[1, place], w[...], 1, 0)
        target[...] = total.astype(target.dtype)


def query_part_kernel(gq, w, wm, part, wkv, wkvf):
    core = lax.axis_index("c")
    flipped = dot(flip_matrix(w.shape[0]), wm[...], 1, 0).astype(BF16)
    wkv[...] = w[:, : 2 * HDIM]
    wkvf[...] = flipped[:, : 2 * HDIM]
    for i, place in enumerate((core, 1 - core)):
        part[i] = dot(gq[0, place], w[:, 2 * HDIM :], 1, 1) + dot(gq[1, place], flipped[:, 2 * HDIM :], 1, 1)


def project_keys(kg, part, wkv, wkvf, keep, send):
    core = lax.axis_index("c")
    for i, (target, place) in enumerate(((keep, core), (send, 1 - core))):
        total = part[i] + dot(kg[0, place], wkv[...], 1, 1) + dot(kg[1, place], wkvf[...], 1, 1)
        target[...] = total.astype(target.dtype)


def key_part_kernel(chosen, dkv, near_p, near_m, far_p, far_m, part, wkv, wkvf, keep, send, kg):
    t = position()
    last = last_block()

    @pl.when(pl.program_id(0) == 0)
    def _():
        for strand in range(2):
            stat_block = last if strand == 0 else 0
            near, far = ((near_p, far_p), (near_m, far_m))[strand]
            for side in range(2):
                for grp in range(2):
                    total = dkv[strand, side, grp]
                    if side != strand:
                        total = total + near[grp].astype(F32)
                        term = far[0, grp].astype(F32)
                        total = total + jnp.where(2 * t + side == stat_block, term, 0.0)
                    dyn_block = chosen[grp] if strand == 0 else last - chosen[grp]
                    term = far[1, grp].astype(F32)
                    total = total + jnp.where(2 * t + side == dyn_block, term, 0.0)
                    kg[strand, side, grp * BLK : (grp + 1) * BLK, :] = total.astype(BF16)

    project_keys(kg, part, wkv, wkvf, keep, send)


def head_group(x, c):
    return x + c * (3 - 2 * x)


def cost(flops, moved):
    return pl.CostEstimate(flops=flops, transcendentals=0, bytes_accessed=moved)


def swap(value, axis):
    return lax.ppermute(value, axis, [(0, 1), (1, 0)])


def after(value, *others):
    return lax.optimization_barrier((value,) + others)[0]


def pair(own, other, index):
    return jnp.where(index == 0, jnp.concatenate([own, other], 0), jnp.concatenate([other, own], 0))


def ring(value, axis):
    count = lax.axis_size(axis)
    return lax.ppermute(value, axis, [(i, (i + 1) % count) for i in range(count)])


def gather_rows(chunk, held):
    na, nb = lax.axis_size("a"), lax.axis_size("b")
    a, b = lax.axis_index("a"), lax.axis_index("b")
    size = chunk.shape[0]
    full = jnp.zeros((na * nb * size, chunk.shape[1]), chunk.dtype)
    across = []
    for step in range(na):
        if 0 < step:
            chunk = ring(after(chunk, *held.get(step, ()), *across[: step - 1][-1:]), "a")
        inner = chunk
        for turn in range(nb):
            pos = ((a - step) % na) * nb + (b - turn) % nb
            full = lax.dynamic_update_slice(full, inner, (pos * size, 0))
            if turn + 1 < nb:
                if step + 1 == na and turn == 0:
                    inner = after(inner, *held.get(-1, ()), *across[-1:])
                inner = ring(inner, "b")
        across.append(inner)
    return full, chunk


def output_rows(w_out, x, a, b, c, held, arrived, kv, awaited):
    na, nb = lax.axis_size("a"), lax.axis_size("b")
    mine = head_group(x, c)
    half = w_out.shape[1] // 2
    if (na, nb) != (4, 2):
        full = lax.all_gather(w_out, ("a", "b", "c"), axis=0, tiled=True)
        rows = REP * HDIM // 2
        place = b % 2
        pieces = []
        for where in (place, 1 - place):
            piece = lax.dynamic_slice(full, (mine * 2 * rows + where * rows, 0), (rows, full.shape[1]))
            pieces += [piece[:, :half], piece[:, half:]]
        return [(piece, jnp.zeros_like(piece)) for piece in pieces]
    source = pair(w_out, swap(w_out, "c"), c)
    current = jnp.where(a == mine, source, 0).astype(source.dtype)

    def spot(x, a, c):
        return (x * na + a) * 2 + c

    def send(value, moves):
        pairs = []
        for (sx, sc), (i, j) in moves.items():
            pairs.append((spot(sx, i, sc), spot(sx, j, sc)))
        return lax.ppermute(value, ("x", "a", "c"), pairs)

    def across(value, holders):
        pairs = []
        for (sx, sc), spots in holders.items():
            for i in spots:
                at = (sx * na + i) * 4 + sc
                pairs += [(at, at + 2), (at + 2, at)]
        return lax.ppermute(value, ("x", "a", "b", "c"), pairs)

    start = after(current, held)
    parts = [start[:, :half], start[:, half:]]
    first = [send(v, {(0, 0): (0, 1), (0, 1): (3, 2), (1, 0): (1, 0), (1, 1): (2, 3)}) for v in parts]
    parts = [after(parts[0] + first[0], kv), after(parts[1] + first[1], arrived[0])]
    second = [send(v, {(0, 0): (1, 2), (0, 1): (2, 1), (1, 0): (1, 2), (1, 1): (2, 1)}) for v in parts]
    early = [across(v, {(0, 0): (0, 1), (0, 1): (3, 2), (1, 0): (1, 0), (1, 1): (2, 3)}) for v in parts]
    third = [
        send(after(v, w, *awaited), {(0, 0): (2, 3), (0, 1): (1, 0), (1, 0): (2, 3), (1, 1): (1, 0)})
        for v, w in zip(second, early)
    ]
    late = [v + w for v, w in zip(second, third)]
    beyond = [across(v, {(0, 0): (2, 3), (0, 1): (1, 0), (1, 0): (2, 3), (1, 1): (1, 0)}) for v in late]
    return list(zip(parts, late)) + list(zip(early, beyond))


def rounds():
    for axis, low in (("b", 1), ("a", lax.axis_size("b"))):
        count = lax.axis_size(axis)
        bit = 1
        while bit < count:
            yield axis, bit * low, [(i, i ^ bit) for i in range(count)]
            bit *= 2


def trade(first, second, t, owner, inward, states, held=(), packed=None):
    for number, (axis, weight, pairs) in enumerate(rounds()):
        if number == 2:
            first = after(first, *held)
        same = (t // weight) % 2 == (owner // weight) % 2
        give = same != inward
        if number > 0 or packed is None:
            packed = jnp.where(give, first, second)
        got = lax.ppermute(packed, axis, pairs)
        states.append(got)
        first, second = jnp.where(give, first, first + got), jnp.where(give, second + got, second)
    return first, second


def body(hidden, w_query, w_keyval, w_out, global_blocks, cotangent):
    x, a, b, c = (lax.axis_index(n) for n in ("x", "a", "b", "c"))
    na, nb = lax.axis_size("a"), lax.axis_size("b")
    n = na * nb
    t = a * nb + b
    blocks = 2 * n
    width = hidden.shape[1]
    mine = head_group(x, c)
    theirs = head_group(x, 1 - c)
    line_up = [(i, i + 1) for i in range(n - 1)]
    line_down = [(i + 1, i) for i in range(n - 1)]

    h10 = swap(hidden, "c")
    h01 = swap(hidden, "x")
    h11 = swap(h01, "c")
    g_own = jnp.sum(global_blocks) - (blocks - 1)
    g_other = swap(after(jnp.full((8, 128), g_own, F32), h01), "x")
    chosen = jnp.stack([g_own, g_other[0, 0].astype(jnp.int32)])
    c10 = swap(cotangent, "c")
    c01 = swap(after(cotangent, g_other), "x")
    c11 = swap(c01, "c")

    half = KVH * HDIM

    def kv_columns(j):
        return jnp.concatenate(
            [
                lax.dynamic_slice_in_dim(w_keyval, j * HDIM, HDIM, 1),
                lax.dynamic_slice_in_dim(w_keyval, half + j * HDIM, HDIM, 1),
            ],
            axis=1,
        )

    def q_columns(j):
        return lax.dynamic_slice_in_dim(w_query, j * REP * HDIM, REP * HDIM, 1)

    normed = pl.pallas_call(
        norm_kernel,
        out_shape=jax.ShapeDtypeStruct((2, 4 * BLK, width), BF16),
        in_specs=[whole()] * 4,
        out_specs=whole(),
        cost_estimate=cost(10**9, 6 * 2**20),
        compiler_params=params(),
        name="norm",
    )(hidden, h01, h10, h11)
    def columns(j):
        return jnp.concatenate([kv_columns(j), q_columns(j)], axis=1)

    held = {3: (h01,), -1: (normed, c01)}
    weight, far_chunk = gather_rows(pair(columns(mine), swap(columns(theirs), "c"), c), held)
    q_weight = weight[:, 2 * HDIM :]
    kv_weight = weight[:, : 2 * HDIM]
    normed = normed.reshape(8 * BLK, width)
    kv = dot(normed, kv_weight, 1, 0).astype(BF16).reshape(2, 2, 2, BLK, 2 * HDIM)

    ctx = ("a", "b")
    up = kv[0, 1]
    down = kv[1, 0]
    near_p, near_m = lax.ppermute(up, ctx, line_up), lax.ppermute(down, ctx, line_down)
    owner = jnp.stack([jnp.full((2,), n - 1, jnp.int32), chosen // 2])
    side = jnp.stack([jnp.ones((2,), jnp.int32), chosen % 2])[:, :, None, None]
    owner = owner[:, :, None, None]
    first = jnp.where(owner == t, jnp.where(side == 0, kv[0, 0], kv[0, 1]), 0).astype(BF16)
    second = jnp.where(n - 1 - owner == t, jnp.where(side == 1, kv[1, 0], kv[1, 1]), 0).astype(BF16)
    first = after(first, c01)
    arrived = []
    first, second = trade(first, second, t, owner, False, arrived)
    wo_parts = output_rows(w_out, x, a, b, c, far_chunk, arrived, kv, ())

    queries = dot(normed, q_weight, 1, 0).astype(BF16).reshape(2, 2, 2, BLK, REP * HDIM)

    grad_att, o_weight = pl.pallas_call(
        grad_att_kernel,
        out_shape=(
            jax.ShapeDtypeStruct((4 * BLK, REP * HDIM), BF16),
            jax.ShapeDtypeStruct((REP * HDIM, width), BF16),
        ),
        in_specs=[whole()] * 12,
        out_specs=[whole()] * 2,
        cost_estimate=cost(10**9, 9 * 2**20),
        compiler_params=params(),
        name="grad_att",
    )(cotangent, c01, c10, c11, *[v for piece in wo_parts for v in piece])
    grad_att = grad_att.reshape(2, 2, BLK, REP * HDIM)

    wide = pl.BlockSpec((2, 2, 1, BLK, REP * HDIM), lambda g: (0, 0, g, 0, 0))
    pairs_spec = pl.BlockSpec((2, 2, 1, BLK, 2 * HDIM), lambda g: (0, 0, g, 0, 0))
    near_spec = pl.BlockSpec((1, BLK, 2 * HDIM), lambda g: (g, 0, 0))
    far_spec = pl.BlockSpec((2, 1, BLK, 2 * HDIM), lambda g: (0, g, 0, 0))
    near_shape = jax.ShapeDtypeStruct((2, BLK, 2 * HDIM), BF16)
    far_shape = jax.ShapeDtypeStruct((2, 2, BLK, 2 * HDIM), BF16)
    extras = [near_spec, near_spec, far_spec, far_spec]
    att, gq, dkv, dnear_p, dnear_m, dfar_p, dfar_m, pack = pl.pallas_call(
        attention_kernel,
        grid=(2,),
        out_shape=(
            jax.ShapeDtypeStruct(queries.shape, BF16),
            jax.ShapeDtypeStruct(queries.shape, BF16),
            jax.ShapeDtypeStruct(kv.shape, F32),
            near_shape,
            near_shape,
            far_shape,
            far_shape,
            far_shape,
        ),
        in_specs=[smem(), wide, pl.BlockSpec((2, 1, BLK, REP * HDIM), lambda g: (0, g, 0, 0)), pairs_spec] + extras,
        out_specs=[wide, wide, pairs_spec] + extras + [far_spec],
        cost_estimate=cost(8 * 10**9, 10 * 2**20),
        compiler_params=params(),
        name="attention",
    )(chosen, queries, grad_att, kv, near_p, near_m, first, second)

    near_p, near_m = lax.ppermute(dnear_p, ctx, line_down), lax.ppermute(dnear_m, ctx, line_up)
    rows = 2 * BLK

    def finish(keep, send):
        got = swap(send, "c")
        other = (keep[BLK:] + got[BLK:].astype(F32)).astype(BF16)
        back = swap(other, "x")
        return keep[:BLK] + got[:BLK].astype(F32) + back.astype(F32), other, back

    chunk = width // 4
    partial = (jax.ShapeDtypeStruct((rows, width), F32), jax.ShapeDtypeStruct((rows, width), BF16))
    out_parts = pl.pallas_call(
            output_kernel,
            grid=(width // chunk,),
            out_shape=partial,
            in_specs=[
                pl.BlockSpec((2, 2, rows, REP * HDIM), lambda k: (0, 0, 0, 0)),
                pl.BlockSpec((REP * HDIM, chunk), lambda k: (0, k)),
            ],
            out_specs=[pl.BlockSpec((rows, chunk), lambda k: (0, k))] * 2,
            cost_estimate=cost(2 * 10**9, 7 * 2**20),
            compiler_params=params(),
            name="output",
        )(att.reshape(2, 2, rows, REP * HDIM), o_weight)
    arrived = []
    far_p, far_m = trade(dfar_p, dfar_m, t, owner, True, arrived, (out_parts[1],), pack)
    total = out_parts[0] + swap(out_parts[1], "c").astype(F32)
    combined_back = swap(total[BLK:].astype(BF16), "x")
    combined = total[:BLK] + combined_back.astype(F32)
    combined = combined.astype(BF16)

    chunk = 256
    steps = width // chunk

    def fixed(shape):
        return pl.BlockSpec(shape, lambda k: (0,) * len(shape))

    part, kv_plain, kv_flipped = pl.pallas_call(
        query_part_kernel,
        grid=(steps,),
        out_shape=(
            jax.ShapeDtypeStruct((2, rows, width), F32),
            jax.ShapeDtypeStruct((width, 2 * HDIM), BF16),
            jax.ShapeDtypeStruct((width, 2 * HDIM), BF16),
        ),
        in_specs=[
            fixed((2, 2, rows, REP * HDIM)),
            pl.BlockSpec((chunk, (2 + REP) * HDIM), lambda k: (k, 0)),
            pl.BlockSpec((chunk, (2 + REP) * HDIM), lambda k: (steps - 1 - k, 0)),
        ],
        out_specs=(
            pl.BlockSpec((2, rows, chunk), lambda k: (0, 0, k)),
            pl.BlockSpec((chunk, 2 * HDIM), lambda k: (k, 0)),
            pl.BlockSpec((chunk, 2 * HDIM), lambda k: (k, 0)),
        ),
        cost_estimate=cost(3 * 10**9, 13 * 2**20),
        compiler_params=params(),
        name="query_part",
    )(after(gq, arrived[1]).reshape(2, 2, rows, REP * HDIM), weight, weight)

    chunk = width // 4
    key_shape = (2, 2, rows, 2 * HDIM)

    def sections(start):
        return [
            pl.BlockSpec((2, rows, chunk), lambda k: (0, 0, k + start)),
            pl.BlockSpec((chunk, 2 * HDIM), lambda k: (k + start, 0)),
            pl.BlockSpec((chunk, 2 * HDIM), lambda k: (k + start, 0)),
        ]

    key_parts = pl.pallas_call(
        key_part_kernel,
        grid=(4,),
        out_shape=partial,
        in_specs=[smem()]
        + [fixed(v) for v in (dkv.shape, near_shape.shape, near_shape.shape)]
        + [fixed(far_shape.shape)] * 2
        + sections(0),
        out_specs=[pl.BlockSpec((rows, chunk), lambda k: (0, k))] * 2,
        scratch_shapes=[pltpu.VMEM(key_shape, BF16)],
        cost_estimate=cost(5 * 10**8, 8 * 2**20),
        compiler_params=params(),
        name="key_part",
    )(chosen, dkv, near_p, near_m, after(far_p, combined_back), far_m, part, kv_plain, kv_flipped)
    grad_norm, _, _ = finish(*key_parts)

    u = hidden.astype(F32)
    inv_rms = lax.rsqrt(jnp.mean(u * u, axis=1, keepdims=True) + EPS)
    scaled = u * inv_rms
    grad_in = inv_rms * (grad_norm - scaled * jnp.mean(grad_norm * scaled, axis=1, keepdims=True))
    return (combined, grad_in.astype(BF16))


def split(count):
    inner = 1
    while (2 * inner) ** 2 <= count:
        inner *= 2
    return count // inner, inner


def solution(mesh):
    na, nb = split(mesh.shape["ctx"] // 2)
    grid = Mesh(mesh.devices.reshape(mesh.shape["groups"], na, nb, 2), ("x", "a", "b", "c"))
    return jax.shard_map(
        body,
        mesh=grid,
        in_specs=(
            P(("x", "a", "b", "c"), None),
            P(("a", "b", "c"), None),
            P(("a", "b", "c"), None),
            P(("a", "b", "c"), None),
            P("x"),
            P(("x", "a", "b", "c"), None),
        ),
        out_specs=(P(("x", "a", "b", "c"), None), P(("x", "a", "b", "c"), None)),
        check_vma=False,
    )
```

```python
import jax
import jax.numpy as jnp
from jax import lax
from jax.experimental import pallas as pl
from jax.experimental.pallas import tpu as pltpu
from jax.sharding import Mesh, PartitionSpec as P

HEADS = 16
KVH = 4
HDIM = 128
BLK = 128
REP = HEADS // KVH
EPS = 1e-05
SCALE = HDIM ** (-0.5)
LOG2E = 1.4426950408889634
F32 = jnp.float32
BF16 = jnp.bfloat16
VMEM = 56 * 1024 * 1024


def dot(a, b, ca, cb):
    return lax.dot_general(a, b, (((ca,), (cb,)), ((), ())), preferred_element_type=F32)


def flip_matrix(n):
    i = lax.broadcasted_iota(jnp.int32, (n, n), 0)
    j = lax.broadcasted_iota(jnp.int32, (n, n), 1)
    return jnp.where(i + j == n - 1, 1.0, 0.0).astype(BF16)


def params():
    return pltpu.CompilerParams(vmem_limit_bytes=VMEM)


def whole():
    return pl.BlockSpec(memory_space=pltpu.VMEM)


def smem():
    return pl.BlockSpec(memory_space=pltpu.SMEM)


def norm_kernel(h00, h01, h10, h11, out):
    core = lax.axis_index("c")
    flip = flip_matrix(128)
    for side, refs in enumerate(((h00, h01), (h10, h11))):
        place = core if side == 0 else 1 - core
        for grp in range(2):
            u = refs[grp][...].astype(F32)
            inv = lax.rsqrt(jnp.mean(u * u, axis=1, keepdims=True) + EPS)
            n = (u * inv).astype(BF16)
            row = pl.multiple_of(place * (2 * BLK) + grp * BLK, BLK)
            out[0, pl.ds(row, BLK), :] = n
            count = n.shape[1] // 128
            for k in range(count):
                m = count - 1 - k
                out[1, pl.ds(row, BLK), m * 128 : m * 128 + 128] = dot(
                    n[:, k * 128 : k * 128 + 128], flip, 1, 0
                ).astype(BF16)


def grad_att_kernel(c00, c01, c10, c11, *refs):
    pieces, (out, w) = refs[:8], refs[8:]
    core = lax.axis_index("c")
    own = lax.axis_index("b") % 2
    half = pieces[0].shape[1]
    rows = pieces[0].shape[0]
    for i in range(4):
        row = pl.multiple_of((own if i < 2 else 1 - own) * rows, rows)
        column = (i % 2) * half
        w[pl.ds(row, rows), column : column + half] = pieces[2 * i][...] + pieces[2 * i + 1][...]
    for side, refs in enumerate(((c00, c01), (c10, c11))):
        place = core if side == 0 else 1 - core
        rows = jnp.concatenate([refs[0][...], refs[1][...]], axis=0)
        row = pl.multiple_of(place * (2 * BLK), 2 * BLK)
        out[pl.ds(row, 2 * BLK), :] = dot(rows, w[...], 1, 1).astype(BF16)


def position():
    return lax.axis_index("a") * lax.axis_size("b") + lax.axis_index("b")


def last_block():
    return 2 * lax.axis_size("a") * lax.axis_size("b") - 1


def attention_kernel(chosen, q, ga, kv, near_p, near_m, far_p, far_m, att, gq, dkv, dnear_p, dnear_m, dfar_p, dfar_m, pack):
    last = last_block()
    t = position()
    g_dyn = chosen[pl.program_id(0)]
    sums = {}

    def load(strand, side):
        near, far = ((near_p, far_p), (near_m, far_m))[strand]
        sets = [kv.at[strand, 0, 0], kv.at[strand, 1, 0], near.at[0], far.at[0, 0], far.at[1, 0]]
        if strand == 0:
            near_set = 2 if side == 0 else 0
        else:
            near_set = 1 if side == 0 else 2
        order = (near_set, side, 3, 4)
        keys = jnp.concatenate([sets[i][:, :HDIM] for i in order], axis=0)
        values = jnp.concatenate([sets[i][:, HDIM:] for i in order], axis=0)
        rows = jnp.concatenate([q[strand, side, 0, :, i * HDIM : (i + 1) * HDIM] for i in range(REP)], axis=0)
        ups = jnp.concatenate([ga[side, 0, :, i * HDIM : (i + 1) * HDIM] for i in range(REP)], axis=0)
        return order, keys, values, rows, ups, dot(rows, keys, 1, 1), dot(ups, values, 1, 1)

    def weigh(strand, side, s, dp):
        block = 2 * t + side
        stat_block = last if strand == 0 else 0
        dyn_block = g_dyn if strand == 0 else last - g_dyn
        next_to = block - 1 if strand == 0 else block + 1
        flags = (
            (next_to >= 0) & (next_to <= last),
            None,
            (stat_block != block) & (stat_block != next_to),
            (dyn_block != block) & (dyn_block != next_to),
        )
        parts = []
        for i in range(4):
            part = s[:, i * BLK : (i + 1) * BLK]
            parts.append(part if flags[i] is None else jnp.where(flags[i], part, -jnp.inf))
        s = jnp.concatenate(parts, axis=1)
        e = jnp.exp2((s - jnp.max(s, axis=1, keepdims=True)) * (SCALE * LOG2E))
        inverse = 1.0 / jnp.sum(e, axis=1, keepdims=True)
        center = jnp.sum(e * dp, axis=1, keepdims=True) * inverse
        p = e * inverse
        return p.astype(BF16), (p * (dp - center)).astype(BF16)

    def emit(strand, side, order, keys, values, rows, ups, ph, ds):
        o = dot(ph, values, 1, 0).astype(BF16)
        dq = (dot(ds, keys, 1, 0) * SCALE).astype(BF16)
        dk = dot(ds, rows, 0, 0) * SCALE
        dv = dot(ph, ups, 0, 0)
        for i in range(REP):
            att[strand, side, 0, :, i * HDIM : (i + 1) * HDIM] = o[i * BLK : (i + 1) * BLK]
            gq[strand, side, 0, :, i * HDIM : (i + 1) * HDIM] = dq[i * BLK : (i + 1) * BLK]
        for i in range(4):
            term = (dk[i * BLK : (i + 1) * BLK], dv[i * BLK : (i + 1) * BLK])
            old = sums.get((strand, order[i]))
            sums[strand, order[i]] = term if old is None else (old[0] + term[0], old[1] + term[1])
        if side == 1:
            dnear, dfar = ((dnear_p, dfar_p), (dnear_m, dfar_m))[strand]
            targets = (dkv.at[strand, 0, 0], dkv.at[strand, 1, 0], dnear.at[0], dfar.at[0, 0], dfar.at[1, 0])
            for i, target in enumerate(targets):
                target[:, :HDIM] = sums[strand, i][0].astype(target.dtype)
                target[:, HDIM:] = sums[strand, i][1].astype(target.dtype)

    units = [(strand, side) for strand in range(2) for side in range(2)]
    following = load(*units[0])
    ready = None
    for number, unit in enumerate(units):
        *held, s, dp = following
        if number + 1 < len(units):
            following = load(*units[number + 1])
        weighed = weigh(*unit, s, dp)
        if ready is not None:
            emit(*ready)
        ready = (*unit, *held, *weighed)
    emit(*ready)

    for i, owner in enumerate((last // 2, g_dyn // 2)):
        pack[i, 0] = jnp.where(t % 2 == owner % 2, dfar_m[i, 0], dfar_p[i, 0])


def output_kernel(att, w, keep, send):
    core = lax.axis_index("c")
    for target, place in ((keep, core), (send, 1 - core)):
        total = dot(att[0, place], w[...], 1, 0) + dot(att[1, place], w[...], 1, 0)
        target[...] = total.astype(target.dtype)


def query_part_kernel(gq, w, wm, part, wkv, wkvf):
    core = lax.axis_index("c")
    flipped = dot(flip_matrix(w.shape[0]), wm[...], 1, 0).astype(BF16)
    wkv[...] = w[:, : 2 * HDIM]
    wkvf[...] = flipped[:, : 2 * HDIM]
    for i, place in enumerate((core, 1 - core)):
        part[i] = dot(gq[0, place], w[:, 2 * HDIM :], 1, 1) + dot(gq[1, place], flipped[:, 2 * HDIM :], 1, 1)


def project_keys(kg, part, wkv, wkvf, keep, send):
    core = lax.axis_index("c")
    for i, (target, place) in enumerate(((keep, core), (send, 1 - core))):
        total = part[i] + dot(kg[0, place], wkv[...], 1, 1) + dot(kg[1, place], wkvf[...], 1, 1)
        target[...] = total.astype(target.dtype)


def key_part_kernel(chosen, dkv, near_p, near_m, far_p, far_m, part, wkv, wkvf, keep, send, kg):
    t = position()
    last = last_block()

    @pl.when(pl.program_id(0) == 0)
    def _():
        for strand in range(2):
            stat_block = last if strand == 0 else 0
            near, far = ((near_p, far_p), (near_m, far_m))[strand]
            for side in range(2):
                for grp in range(2):
                    total = dkv[strand, side, grp]
                    if side != strand:
                        total = total + near[grp].astype(F32)
                        term = far[0, grp].astype(F32)
                        total = total + jnp.where(2 * t + side == stat_block, term, 0.0)
                    dyn_block = chosen[grp] if strand == 0 else last - chosen[grp]
                    term = far[1, grp].astype(F32)
                    total = total + jnp.where(2 * t + side == dyn_block, term, 0.0)
                    kg[strand, side, grp * BLK : (grp + 1) * BLK, :] = total.astype(BF16)

    project_keys(kg, part, wkv, wkvf, keep, send)


def head_group(x, c):
    return x + c * (3 - 2 * x)


def cost(flops, moved):
    return pl.CostEstimate(flops=flops, transcendentals=0, bytes_accessed=moved)


def swap(value, axis):
    return lax.ppermute(value, axis, [(0, 1), (1, 0)])


def after(value, *others):
    return lax.optimization_barrier((value,) + others)[0]


def pair(own, other, index):
    return jnp.where(index == 0, jnp.concatenate([own, other], 0), jnp.concatenate([other, own], 0))


def ring(value, axis):
    count = lax.axis_size(axis)
    return lax.ppermute(value, axis, [(i, (i + 1) % count) for i in range(count)])


def gather_rows(chunk, held):
    na, nb = lax.axis_size("a"), lax.axis_size("b")
    a, b = lax.axis_index("a"), lax.axis_index("b")
    size = chunk.shape[0]
    full = jnp.zeros((na * nb * size, chunk.shape[1]), chunk.dtype)
    across = []
    for step in range(na):
        if 0 < step:
            chunk = ring(after(chunk, *held.get(step, ()), *across[: step - 1][-1:]), "a")
        inner = chunk
        for turn in range(nb):
            pos = ((a - step) % na) * nb + (b - turn) % nb
            full = lax.dynamic_update_slice(full, inner, (pos * size, 0))
            if turn + 1 < nb:
                if step + 1 == na and turn == 0:
                    inner = after(inner, *held.get(-1, ()), *across[-1:])
                inner = ring(inner, "b")
        across.append(inner)
    return full, chunk


def output_rows(w_out, x, a, b, c, held, arrived, kv, awaited):
    na, nb = lax.axis_size("a"), lax.axis_size("b")
    mine = head_group(x, c)
    half = w_out.shape[1] // 2
    if (na, nb) != (4, 2):
        full = lax.all_gather(w_out, ("a", "b", "c"), axis=0, tiled=True)
        rows = REP * HDIM // 2
        place = b % 2
        pieces = []
        for where in (place, 1 - place):
            piece = lax.dynamic_slice(full, (mine * 2 * rows + where * rows, 0), (rows, full.shape[1]))
            pieces += [piece[:, :half], piece[:, half:]]
        return [(piece, jnp.zeros_like(piece)) for piece in pieces]
    source = pair(w_out, swap(w_out, "c"), c)
    current = jnp.where(a == mine, source, 0).astype(source.dtype)

    def spot(x, a, c):
        return (x * na + a) * 2 + c

    def send(value, moves):
        pairs = []
        for (sx, sc), (i, j) in moves.items():
            pairs.append((spot(sx, i, sc), spot(sx, j, sc)))
        return lax.ppermute(value, ("x", "a", "c"), pairs)

    def across(value, holders):
        pairs = []
        for (sx, sc), spots in holders.items():
            for i in spots:
                at = (sx * na + i) * 4 + sc
                pairs += [(at, at + 2), (at + 2, at)]
        return lax.ppermute(value, ("x", "a", "b", "c"), pairs)

    start = after(current, held)
    parts = [start[:, :half], start[:, half:]]
    first = [send(v, {(0, 0): (0, 1), (0, 1): (3, 2), (1, 0): (1, 0), (1, 1): (2, 3)}) for v in parts]
    parts = [after(parts[0] + first[0], kv), after(parts[1] + first[1], arrived[0])]
    second = [send(v, {(0, 0): (1, 2), (0, 1): (2, 1), (1, 0): (1, 2), (1, 1): (2, 1)}) for v in parts]
    early = [across(v, {(0, 0): (0, 1), (0, 1): (3, 2), (1, 0): (1, 0), (1, 1): (2, 3)}) for v in parts]
    third = [
        send(after(v, w, *awaited), {(0, 0): (2, 3), (0, 1): (1, 0), (1, 0): (2, 3), (1, 1): (1, 0)})
        for v, w in zip(second, early)
    ]
    late = [v + w for v, w in zip(second, third)]
    beyond = [across(v, {(0, 0): (2, 3), (0, 1): (1, 0), (1, 0): (2, 3), (1, 1): (1, 0)}) for v in late]
    return list(zip(parts, late)) + list(zip(early, beyond))


def rounds():
    for axis, low in (("b", 1), ("a", lax.axis_size("b"))):
        count = lax.axis_size(axis)
        bit = 1
        while bit < count:
            yield axis, bit * low, [(i, i ^ bit) for i in range(count)]
            bit *= 2


def trade(first, second, t, owner, inward, states, held=(), packed=None):
    for number, (axis, weight, pairs) in enumerate(rounds()):
        if number == 2:
            first = after(first, *held)
        same = (t // weight) % 2 == (owner // weight) % 2
        give = same != inward
        if number > 0 or packed is None:
            packed = jnp.where(give, first, second)
        got = lax.ppermute(packed, axis, pairs)
        states.append(got)
        first, second = jnp.where(give, first, first + got), jnp.where(give, second + got, second)
    return first, second


def body(hidden, w_query, w_keyval, w_out, global_blocks, cotangent):
    x, a, b, c = (lax.axis_index(n) for n in ("x", "a", "b", "c"))
    na, nb = lax.axis_size("a"), lax.axis_size("b")
    n = na * nb
    t = a * nb + b
    blocks = 2 * n
    width = hidden.shape[1]
    mine = head_group(x, c)
    theirs = head_group(x, 1 - c)
    line_up = [(i, i + 1) for i in range(n - 1)]
    line_down = [(i + 1, i) for i in range(n - 1)]

    h10 = swap(hidden, "c")
    h01 = swap(hidden, "x")
    h11 = swap(h01, "c")
    g_own = jnp.sum(global_blocks) - (blocks - 1)
    g_other = swap(after(jnp.full((8, 128), g_own, F32), h01), "x")
    chosen = jnp.stack([g_own, g_other[0, 0].astype(jnp.int32)])
    c10 = swap(cotangent, "c")
    c01 = swap(after(cotangent, g_other), "x")
    c11 = swap(c01, "c")

    half = KVH * HDIM

    def kv_columns(j):
        return jnp.concatenate(
            [
                lax.dynamic_slice_in_dim(w_keyval, j * HDIM, HDIM, 1),
                lax.dynamic_slice_in_dim(w_keyval, half + j * HDIM, HDIM, 1),
            ],
            axis=1,
        )

    def q_columns(j):
        return lax.dynamic_slice_in_dim(w_query, j * REP * HDIM, REP * HDIM, 1)

    normed = pl.pallas_call(
        norm_kernel,
        out_shape=jax.ShapeDtypeStruct((2, 4 * BLK, width), BF16),
        in_specs=[whole()] * 4,
        out_specs=whole(),
        cost_estimate=cost(10**9, 6 * 2**20),
        compiler_params=params(),
        name="norm",
    )(hidden, h01, h10, h11)
    def columns(j):
        return jnp.concatenate([kv_columns(j), q_columns(j)], axis=1)

    held = {3: (h01,), -1: (normed, c01)}
    weight, far_chunk = gather_rows(pair(columns(mine), swap(columns(theirs), "c"), c), held)
    q_weight = weight[:, 2 * HDIM :]
    kv_weight = weight[:, : 2 * HDIM]
    normed = normed.reshape(8 * BLK, width)
    kv = dot(normed, kv_weight, 1, 0).astype(BF16).reshape(2, 2, 2, BLK, 2 * HDIM)

    ctx = ("a", "b")
    up = kv[0, 1]
    down = kv[1, 0]
    near_p, near_m = lax.ppermute(up, ctx, line_up), lax.ppermute(down, ctx, line_down)
    owner = jnp.stack([jnp.full((2,), n - 1, jnp.int32), chosen // 2])
    side = jnp.stack([jnp.ones((2,), jnp.int32), chosen % 2])[:, :, None, None]
    owner = owner[:, :, None, None]
    first = jnp.where(owner == t, jnp.where(side == 0, kv[0, 0], kv[0, 1]), 0).astype(BF16)
    second = jnp.where(n - 1 - owner == t, jnp.where(side == 1, kv[1, 0], kv[1, 1]), 0).astype(BF16)
    first = after(first, c01)
    arrived = []
    first, second = trade(first, second, t, owner, False, arrived)
    wo_parts = output_rows(w_out, x, a, b, c, far_chunk, arrived, kv, ())

    queries = dot(normed, q_weight, 1, 0).astype(BF16).reshape(2, 2, 2, BLK, REP * HDIM)

    grad_att, o_weight = pl.pallas_call(
        grad_att_kernel,
        out_shape=(
            jax.ShapeDtypeStruct((4 * BLK, REP * HDIM), BF16),
            jax.ShapeDtypeStruct((REP * HDIM, width), BF16),
        ),
        in_specs=[whole()] * 12,
        out_specs=[whole()] * 2,
        cost_estimate=cost(10**9, 9 * 2**20),
        compiler_params=params(),
        name="grad_att",
    )(cotangent, c01, c10, c11, *[v for piece in wo_parts for v in piece])
    grad_att = grad_att.reshape(2, 2, BLK, REP * HDIM)

    wide = pl.BlockSpec((2, 2, 1, BLK, REP * HDIM), lambda g: (0, 0, g, 0, 0))
    pairs_spec = pl.BlockSpec((2, 2, 1, BLK, 2 * HDIM), lambda g: (0, 0, g, 0, 0))
    near_spec = pl.BlockSpec((1, BLK, 2 * HDIM), lambda g: (g, 0, 0))
    far_spec = pl.BlockSpec((2, 1, BLK, 2 * HDIM), lambda g: (0, g, 0, 0))
    near_shape = jax.ShapeDtypeStruct((2, BLK, 2 * HDIM), BF16)
    far_shape = jax.ShapeDtypeStruct((2, 2, BLK, 2 * HDIM), BF16)
    extras = [near_spec, near_spec, far_spec, far_spec]
    att, gq, dkv, dnear_p, dnear_m, dfar_p, dfar_m, pack = pl.pallas_call(
        attention_kernel,
        grid=(2,),
        out_shape=(
            jax.ShapeDtypeStruct(queries.shape, BF16),
            jax.ShapeDtypeStruct(queries.shape, BF16),
            jax.ShapeDtypeStruct(kv.shape, F32),
            near_shape,
            near_shape,
            far_shape,
            far_shape,
            far_shape,
        ),
        in_specs=[smem(), wide, pl.BlockSpec((2, 1, BLK, REP * HDIM), lambda g: (0, g, 0, 0)), pairs_spec] + extras,
        out_specs=[wide, wide, pairs_spec] + extras + [far_spec],
        cost_estimate=cost(8 * 10**9, 10 * 2**20),
        compiler_params=params(),
        name="attention",
    )(chosen, queries, grad_att, kv, near_p, near_m, first, second)

    near_p, near_m = lax.ppermute(dnear_p, ctx, line_down), lax.ppermute(dnear_m, ctx, line_up)
    rows = 2 * BLK

    def finish(keep, send):
        got = swap(send, "c")
        other = (keep[BLK:] + got[BLK:].astype(F32)).astype(BF16)
        back = swap(other, "x")
        return keep[:BLK] + got[:BLK].astype(F32) + back.astype(F32), other, back

    chunk = width // 4
    partial = (jax.ShapeDtypeStruct((rows, width), F32), jax.ShapeDtypeStruct((rows, width), BF16))
    out_parts = pl.pallas_call(
            output_kernel,
            grid=(width // chunk,),
            out_shape=partial,
            in_specs=[
                pl.BlockSpec((2, 2, rows, REP * HDIM), lambda k: (0, 0, 0, 0)),
                pl.BlockSpec((REP * HDIM, chunk), lambda k: (0, k)),
            ],
            out_specs=[pl.BlockSpec((rows, chunk), lambda k: (0, k))] * 2,
            cost_estimate=cost(2 * 10**9, 7 * 2**20),
            compiler_params=params(),
            name="output",
        )(att.reshape(2, 2, rows, REP * HDIM), o_weight)
    arrived = []
    far_p, far_m = trade(dfar_p, dfar_m, t, owner, True, arrived, (out_parts[1],), pack)
    total = out_parts[0] + swap(out_parts[1], "c").astype(F32)
    combined_back = swap(total[BLK:].astype(BF16), "x")
    combined = total[:BLK] + combined_back.astype(F32)
    combined = combined.astype(BF16)

    chunk = 256
    steps = width // chunk

    def fixed(shape):
        return pl.BlockSpec(shape, lambda k: (0,) * len(shape))

    part, kv_plain, kv_flipped = pl.pallas_call(
        query_part_kernel,
        grid=(steps,),
        out_shape=(
            jax.ShapeDtypeStruct((2, rows, width), F32),
            jax.ShapeDtypeStruct((width, 2 * HDIM), BF16),
            jax.ShapeDtypeStruct((width, 2 * HDIM), BF16),
        ),
        in_specs=[
            fixed((2, 2, rows, REP * HDIM)),
            pl.BlockSpec((chunk, (2 + REP) * HDIM), lambda k: (k, 0)),
            pl.BlockSpec((chunk, (2 + REP) * HDIM), lambda k: (steps - 1 - k, 0)),
        ],
        out_specs=(
            pl.BlockSpec((2, rows, chunk), lambda k: (0, 0, k)),
            pl.BlockSpec((chunk, 2 * HDIM), lambda k: (k, 0)),
            pl.BlockSpec((chunk, 2 * HDIM), lambda k: (k, 0)),
        ),
        cost_estimate=cost(3 * 10**9, 13 * 2**20),
        compiler_params=params(),
        name="query_part",
    )(after(gq, arrived[1]).reshape(2, 2, rows, REP * HDIM), weight, weight)

    chunk = width // 2
    key_shape = (2, 2, rows, 2 * HDIM)

    def sections(start):
        return [
            pl.BlockSpec((2, rows, chunk), lambda k: (0, 0, k + start)),
            pl.BlockSpec((chunk, 2 * HDIM), lambda k: (k + start, 0)),
            pl.BlockSpec((chunk, 2 * HDIM), lambda k: (k + start, 0)),
        ]

    key_parts = pl.pallas_call(
        key_part_kernel,
        grid=(2,),
        out_shape=partial,
        in_specs=[smem()]
        + [fixed(v) for v in (dkv.shape, near_shape.shape, near_shape.shape)]
        + [fixed(far_shape.shape)] * 2
        + sections(0),
        out_specs=[pl.BlockSpec((rows, chunk), lambda k: (0, k))] * 2,
        scratch_shapes=[pltpu.VMEM(key_shape, BF16)],
        cost_estimate=cost(5 * 10**8, 8 * 2**20),
        compiler_params=params(),
        name="key_part",
    )(chosen, dkv, near_p, near_m, after(far_p, combined_back), far_m, part, kv_plain, kv_flipped)
    grad_norm, _, _ = finish(*key_parts)

    u = hidden.astype(F32)
    inv_rms = lax.rsqrt(jnp.mean(u * u, axis=1, keepdims=True) + EPS)
    scaled = u * inv_rms
    grad_in = inv_rms * (grad_norm - scaled * jnp.mean(grad_norm * scaled, axis=1, keepdims=True))
    return (combined, grad_in.astype(BF16))


def split(count):
    inner = 1
    while (2 * inner) ** 2 <= count:
        inner *= 2
    return count // inner, inner


def solution(mesh):
    na, nb = split(mesh.shape["ctx"] // 2)
    grid = Mesh(mesh.devices.reshape(mesh.shape["groups"], na, nb, 2), ("x", "a", "b", "c"))
    return jax.shard_map(
        body,
        mesh=grid,
        in_specs=(
            P(("x", "a", "b", "c"), None),
            P(("a", "b", "c"), None),
            P(("a", "b", "c"), None),
            P(("a", "b", "c"), None),
            P("x"),
            P(("x", "a", "b", "c"), None),
        ),
        out_specs=(P(("x", "a", "b", "c"), None), P(("x", "a", "b", "c"), None)),
        check_vma=False,
    )
```

```python
import jax
import jax.numpy as jnp
from jax import lax
from jax.experimental import pallas as pl
from jax.experimental.pallas import tpu as pltpu
from jax.sharding import Mesh, PartitionSpec as P

HEADS = 16
KVH = 4
HDIM = 128
BLK = 128
REP = HEADS // KVH
EPS = 1e-05
SCALE = HDIM ** (-0.5)
LOG2E = 1.4426950408889634
F32 = jnp.float32
BF16 = jnp.bfloat16
VMEM = 56 * 1024 * 1024


def dot(a, b, ca, cb):
    return lax.dot_general(a, b, (((ca,), (cb,)), ((), ())), preferred_element_type=F32)


def flip_matrix(n):
    i = lax.broadcasted_iota(jnp.int32, (n, n), 0)
    j = lax.broadcasted_iota(jnp.int32, (n, n), 1)
    return jnp.where(i + j == n - 1, 1.0, 0.0).astype(BF16)


def params():
    return pltpu.CompilerParams(vmem_limit_bytes=VMEM)


def whole():
    return pl.BlockSpec(memory_space=pltpu.VMEM)


def smem():
    return pl.BlockSpec(memory_space=pltpu.SMEM)


def norm_kernel(h00, h01, h10, h11, out):
    core = lax.axis_index("c")
    flip = flip_matrix(128)
    for side, refs in enumerate(((h00, h01), (h10, h11))):
        place = core if side == 0 else 1 - core
        for grp in range(2):
            u = refs[grp][...].astype(F32)
            inv = lax.rsqrt(jnp.mean(u * u, axis=1, keepdims=True) + EPS)
            n = (u * inv).astype(BF16)
            row = pl.multiple_of(place * (2 * BLK) + grp * BLK, BLK)
            out[0, pl.ds(row, BLK), :] = n
            count = n.shape[1] // 128
            for k in range(count):
                m = count - 1 - k
                out[1, pl.ds(row, BLK), m * 128 : m * 128 + 128] = dot(
                    n[:, k * 128 : k * 128 + 128], flip, 1, 0
                ).astype(BF16)


def grad_att_kernel(c00, c01, c10, c11, *refs):
    pieces, (out, w) = refs[:8], refs[8:]
    core = lax.axis_index("c")
    own = lax.axis_index("b") % 2
    half = pieces[0].shape[1]
    rows = pieces[0].shape[0]
    for i in range(4):
        row = pl.multiple_of((own if i < 2 else 1 - own) * rows, rows)
        column = (i % 2) * half
        w[pl.ds(row, rows), column : column + half] = pieces[2 * i][...] + pieces[2 * i + 1][...]
    for side, refs in enumerate(((c00, c01), (c10, c11))):
        place = core if side == 0 else 1 - core
        rows = jnp.concatenate([refs[0][...], refs[1][...]], axis=0)
        row = pl.multiple_of(place * (2 * BLK), 2 * BLK)
        out[pl.ds(row, 2 * BLK), :] = dot(rows, w[...], 1, 1).astype(BF16)


def position():
    return lax.axis_index("a") * lax.axis_size("b") + lax.axis_index("b")


def last_block():
    return 2 * lax.axis_size("a") * lax.axis_size("b") - 1


def attention_kernel(chosen, q, ga, kv, near_p, near_m, far_p, far_m, att, gq, dkv, dnear_p, dnear_m, dfar_p, dfar_m, pack):
    last = last_block()
    t = position()
    g_dyn = chosen[pl.program_id(0)]
    sums = {}

    def load(strand, side):
        near, far = ((near_p, far_p), (near_m, far_m))[strand]
        sets = [kv.at[strand, 0, 0], kv.at[strand, 1, 0], near.at[0], far.at[0, 0], far.at[1, 0]]
        if strand == 0:
            near_set = 2 if side == 0 else 0
        else:
            near_set = 1 if side == 0 else 2
        order = (near_set, side, 3, 4)
        keys = jnp.concatenate([sets[i][:, :HDIM] for i in order], axis=0)
        values = jnp.concatenate([sets[i][:, HDIM:] for i in order], axis=0)
        rows = jnp.concatenate([q[strand, side, 0, :, i * HDIM : (i + 1) * HDIM] for i in range(REP)], axis=0)
        ups = jnp.concatenate([ga[side, 0, :, i * HDIM : (i + 1) * HDIM] for i in range(REP)], axis=0)
        return order, keys, values, rows, ups, dot(rows, keys, 1, 1), dot(ups, values, 1, 1)

    def weigh(strand, side, s, dp):
        block = 2 * t + side
        stat_block = last if strand == 0 else 0
        dyn_block = g_dyn if strand == 0 else last - g_dyn
        next_to = block - 1 if strand == 0 else block + 1
        flags = (
            (next_to >= 0) & (next_to <= last),
            None,
            (stat_block != block) & (stat_block != next_to),
            (dyn_block != block) & (dyn_block != next_to),
        )
        parts = []
        for i in range(4):
            part = s[:, i * BLK : (i + 1) * BLK]
            parts.append(part if flags[i] is None else jnp.where(flags[i], part, -jnp.inf))
        s = jnp.concatenate(parts, axis=1)
        e = jnp.exp2((s - jnp.max(s, axis=1, keepdims=True)) * (SCALE * LOG2E))
        inverse = 1.0 / jnp.sum(e, axis=1, keepdims=True)
        center = jnp.sum(e * dp, axis=1, keepdims=True) * inverse
        p = e * inverse
        return p.astype(BF16), (p * (dp - center)).astype(BF16)

    def emit(strand, side, order, keys, values, rows, ups, ph, ds):
        o = dot(ph, values, 1, 0).astype(BF16)
        dq = (dot(ds, keys, 1, 0) * SCALE).astype(BF16)
        dk = dot(ds, rows, 0, 0) * SCALE
        dv = dot(ph, ups, 0, 0)
        for i in range(REP):
            att[strand, side, 0, :, i * HDIM : (i + 1) * HDIM] = o[i * BLK : (i + 1) * BLK]
            gq[strand, side, 0, :, i * HDIM : (i + 1) * HDIM] = dq[i * BLK : (i + 1) * BLK]
        for i in range(4):
            term = (dk[i * BLK : (i + 1) * BLK], dv[i * BLK : (i + 1) * BLK])
            old = sums.get((strand, order[i]))
            sums[strand, order[i]] = term if old is None else (old[0] + term[0], old[1] + term[1])
        if side == 1:
            dnear, dfar = ((dnear_p, dfar_p), (dnear_m, dfar_m))[strand]
            targets = (dkv.at[strand, 0, 0], dkv.at[strand, 1, 0], dnear.at[0], dfar.at[0, 0], dfar.at[1, 0])
            for i, target in enumerate(targets):
                target[:, :HDIM] = sums[strand, i][0].astype(target.dtype)
                target[:, HDIM:] = sums[strand, i][1].astype(target.dtype)

    units = [(strand, side) for strand in range(2) for side in range(2)]
    following = load(*units[0])
    ready = None
    for number, unit in enumerate(units):
        *held, s, dp = following
        if number + 1 < len(units):
            following = load(*units[number + 1])
        weighed = weigh(*unit, s, dp)
        if ready is not None:
            emit(*ready)
        ready = (*unit, *held, *weighed)
    emit(*ready)

    for i, owner in enumerate((last // 2, g_dyn // 2)):
        pack[i, 0] = jnp.where(t % 2 == owner % 2, dfar_m[i, 0], dfar_p[i, 0])


def output_kernel(att, w, keep, send):
    core = lax.axis_index("c")
    for target, place in ((keep, core), (send, 1 - core)):
        total = dot(att[0, place], w[...], 1, 0) + dot(att[1, place], w[...], 1, 0)
        target[...] = total.astype(target.dtype)


def query_part_kernel(gq, w, wm, part, wkv, wkvf):
    core = lax.axis_index("c")
    flipped = dot(flip_matrix(w.shape[0]), wm[...], 1, 0).astype(BF16)
    wkv[...] = w[:, : 2 * HDIM]
    wkvf[...] = flipped[:, : 2 * HDIM]
    for i, place in enumerate((core, 1 - core)):
        part[i] = dot(gq[0, place], w[:, 2 * HDIM :], 1, 1) + dot(gq[1, place], flipped[:, 2 * HDIM :], 1, 1)


def project_keys(kg, part, wkv, wkvf, keep, send):
    core = lax.axis_index("c")
    for i, (target, place) in enumerate(((keep, core), (send, 1 - core))):
        total = part[i] + dot(kg[0, place], wkv[...], 1, 1) + dot(kg[1, place], wkvf[...], 1, 1)
        target[...] = total.astype(target.dtype)


def key_part_kernel(chosen, dkv, near_p, near_m, far_p, far_m, part, wkv, wkvf, keep, send, kg):
    t = position()
    last = last_block()

    @pl.when(pl.program_id(0) == 0)
    def _():
        for strand in range(2):
            stat_block = last if strand == 0 else 0
            near, far = ((near_p, far_p), (near_m, far_m))[strand]
            for side in range(2):
                for grp in range(2):
                    total = dkv[strand, side, grp]
                    if side != strand:
                        total = total + near[grp].astype(F32)
                        term = far[0, grp].astype(F32)
                        total = total + jnp.where(2 * t + side == stat_block, term, 0.0)
                    dyn_block = chosen[grp] if strand == 0 else last - chosen[grp]
                    term = far[1, grp].astype(F32)
                    total = total + jnp.where(2 * t + side == dyn_block, term, 0.0)
                    kg[strand, side, grp * BLK : (grp + 1) * BLK, :] = total.astype(BF16)

    project_keys(kg, part, wkv, wkvf, keep, send)


def head_group(x, c):
    return x + c * (3 - 2 * x)


def cost(flops, moved):
    return pl.CostEstimate(flops=flops, transcendentals=0, bytes_accessed=moved)


def swap(value, axis):
    return lax.ppermute(value, axis, [(0, 1), (1, 0)])


def after(value, *others):
    return lax.optimization_barrier((value,) + others)[0]


def pair(own, other, index):
    return jnp.where(index == 0, jnp.concatenate([own, other], 0), jnp.concatenate([other, own], 0))


def ring(value, axis):
    count = lax.axis_size(axis)
    return lax.ppermute(value, axis, [(i, (i + 1) % count) for i in range(count)])


def gather_rows(chunk, held):
    na, nb = lax.axis_size("a"), lax.axis_size("b")
    a, b = lax.axis_index("a"), lax.axis_index("b")
    size = chunk.shape[0]
    full = jnp.zeros((na * nb * size, chunk.shape[1]), chunk.dtype)
    across = []
    for step in range(na):
        if 0 < step:
            chunk = ring(after(chunk, *held.get(step, ()), *across[: step - 1][-1:]), "a")
        inner = chunk
        for turn in range(nb):
            pos = ((a - step) % na) * nb + (b - turn) % nb
            full = lax.dynamic_update_slice(full, inner, (pos * size, 0))
            if turn + 1 < nb:
                if step + 1 == na and turn == 0:
                    inner = after(inner, *held.get(-1, ()), *across[-1:])
                inner = ring(inner, "b")
        across.append(inner)
    return full, chunk


def output_rows(w_out, x, a, b, c, held, arrived, kv, awaited):
    na, nb = lax.axis_size("a"), lax.axis_size("b")
    mine = head_group(x, c)
    half = w_out.shape[1] // 2
    if (na, nb) != (4, 2):
        full = lax.all_gather(w_out, ("a", "b", "c"), axis=0, tiled=True)
        rows = REP * HDIM // 2
        place = b % 2
        pieces = []
        for where in (place, 1 - place):
            piece = lax.dynamic_slice(full, (mine * 2 * rows + where * rows, 0), (rows, full.shape[1]))
            pieces += [piece[:, :half], piece[:, half:]]
        return [(piece, jnp.zeros_like(piece)) for piece in pieces]
    source = pair(w_out, swap(w_out, "c"), c)
    current = jnp.where(a == mine, source, 0).astype(source.dtype)

    def spot(x, a, c):
        return (x * na + a) * 2 + c

    def send(value, moves):
        pairs = []
        for (sx, sc), (i, j) in moves.items():
            pairs.append((spot(sx, i, sc), spot(sx, j, sc)))
        return lax.ppermute(value, ("x", "a", "c"), pairs)

    def across(value, holders):
        pairs = []
        for (sx, sc), spots in holders.items():
            for i in spots:
                at = (sx * na + i) * 4 + sc
                pairs += [(at, at + 2), (at + 2, at)]
        return lax.ppermute(value, ("x", "a", "b", "c"), pairs)

    start = after(current, held)
    parts = [start[:, :half], start[:, half:]]
    first = [send(v, {(0, 0): (0, 1), (0, 1): (3, 2), (1, 0): (1, 0), (1, 1): (2, 3)}) for v in parts]
    parts = [after(parts[0] + first[0], kv), after(parts[1] + first[1], arrived[0])]
    second = [send(v, {(0, 0): (1, 2), (0, 1): (2, 1), (1, 0): (1, 2), (1, 1): (2, 1)}) for v in parts]
    early = [across(v, {(0, 0): (0, 1), (0, 1): (3, 2), (1, 0): (1, 0), (1, 1): (2, 3)}) for v in parts]
    third = [
        send(after(v, w, *awaited), {(0, 0): (2, 3), (0, 1): (1, 0), (1, 0): (2, 3), (1, 1): (1, 0)})
        for v, w in zip(second, early)
    ]
    late = [v + w for v, w in zip(second, third)]
    beyond = [across(v, {(0, 0): (2, 3), (0, 1): (1, 0), (1, 0): (2, 3), (1, 1): (1, 0)}) for v in late]
    return list(zip(parts, late)) + list(zip(early, beyond))


def rounds():
    for axis, low in (("b", 1), ("a", lax.axis_size("b"))):
        count = lax.axis_size(axis)
        bit = 1
        while bit < count:
            yield axis, bit * low, [(i, i ^ bit) for i in range(count)]
            bit *= 2


def trade(first, second, t, owner, inward, states, held=(), packed=None):
    for number, (axis, weight, pairs) in enumerate(rounds()):
        if number == 2:
            first = after(first, *held)
        same = (t // weight) % 2 == (owner // weight) % 2
        give = same != inward
        if number > 0 or packed is None:
            packed = jnp.where(give, first, second)
        got = lax.ppermute(packed, axis, pairs)
        states.append(got)
        first, second = jnp.where(give, first, first + got), jnp.where(give, second + got, second)
    return first, second


def body(hidden, w_query, w_keyval, w_out, global_blocks, cotangent):
    x, a, b, c = (lax.axis_index(n) for n in ("x", "a", "b", "c"))
    na, nb = lax.axis_size("a"), lax.axis_size("b")
    n = na * nb
    t = a * nb + b
    blocks = 2 * n
    width = hidden.shape[1]
    mine = head_group(x, c)
    theirs = head_group(x, 1 - c)
    line_up = [(i, i + 1) for i in range(n - 1)]
    line_down = [(i + 1, i) for i in range(n - 1)]

    h10 = swap(hidden, "c")
    h01 = swap(hidden, "x")
    h11 = swap(h01, "c")
    g_own = jnp.sum(global_blocks) - (blocks - 1)
    g_other = swap(after(jnp.full((8, 128), g_own, F32), h01), "x")
    chosen = jnp.stack([g_own, g_other[0, 0].astype(jnp.int32)])
    c10 = swap(cotangent, "c")
    c01 = swap(after(cotangent, g_other), "x")
    c11 = swap(c01, "c")

    half = KVH * HDIM

    def kv_columns(j):
        return jnp.concatenate(
            [
                lax.dynamic_slice_in_dim(w_keyval, j * HDIM, HDIM, 1),
                lax.dynamic_slice_in_dim(w_keyval, half + j * HDIM, HDIM, 1),
            ],
            axis=1,
        )

    def q_columns(j):
        return lax.dynamic_slice_in_dim(w_query, j * REP * HDIM, REP * HDIM, 1)

    normed = pl.pallas_call(
        norm_kernel,
        out_shape=jax.ShapeDtypeStruct((2, 4 * BLK, width), BF16),
        in_specs=[whole()] * 4,
        out_specs=whole(),
        cost_estimate=cost(10**9, 6 * 2**20),
        compiler_params=params(),
        name="norm",
    )(hidden, h01, h10, h11)
    def columns(j):
        return jnp.concatenate([kv_columns(j), q_columns(j)], axis=1)

    held = {3: (h01,), -1: (normed, c01)}
    weight, far_chunk = gather_rows(pair(columns(mine), swap(columns(theirs), "c"), c), held)
    q_weight = weight[:, 2 * HDIM :]
    kv_weight = weight[:, : 2 * HDIM]
    normed = normed.reshape(8 * BLK, width)
    kv = dot(normed, kv_weight, 1, 0).astype(BF16).reshape(2, 2, 2, BLK, 2 * HDIM)

    ctx = ("a", "b")
    up = kv[0, 1]
    down = kv[1, 0]
    near_p, near_m = lax.ppermute(up, ctx, line_up), lax.ppermute(down, ctx, line_down)
    owner = jnp.stack([jnp.full((2,), n - 1, jnp.int32), chosen // 2])
    side = jnp.stack([jnp.ones((2,), jnp.int32), chosen % 2])[:, :, None, None]
    owner = owner[:, :, None, None]
    first = jnp.where(owner == t, jnp.where(side == 0, kv[0, 0], kv[0, 1]), 0).astype(BF16)
    second = jnp.where(n - 1 - owner == t, jnp.where(side == 1, kv[1, 0], kv[1, 1]), 0).astype(BF16)
    first = after(first, c01)
    arrived = []
    first, second = trade(first, second, t, owner, False, arrived)
    wo_parts = output_rows(w_out, x, a, b, c, far_chunk, arrived, kv, ())

    queries = dot(normed, q_weight, 1, 0).astype(BF16).reshape(2, 2, 2, BLK, REP * HDIM)

    grad_att, o_weight = pl.pallas_call(
        grad_att_kernel,
        out_shape=(
            jax.ShapeDtypeStruct((4 * BLK, REP * HDIM), BF16),
            jax.ShapeDtypeStruct((REP * HDIM, width), BF16),
        ),
        in_specs=[whole()] * 12,
        out_specs=[whole()] * 2,
        cost_estimate=cost(10**9, 9 * 2**20),
        compiler_params=params(),
        name="grad_att",
    )(cotangent, c01, c10, c11, *[v for piece in wo_parts for v in piece])
    grad_att = grad_att.reshape(2, 2, BLK, REP * HDIM)

    wide = pl.BlockSpec((2, 2, 1, BLK, REP * HDIM), lambda g: (0, 0, g, 0, 0))
    pairs_spec = pl.BlockSpec((2, 2, 1, BLK, 2 * HDIM), lambda g: (0, 0, g, 0, 0))
    near_spec = pl.BlockSpec((1, BLK, 2 * HDIM), lambda g: (g, 0, 0))
    far_spec = pl.BlockSpec((2, 1, BLK, 2 * HDIM), lambda g: (0, g, 0, 0))
    near_shape = jax.ShapeDtypeStruct((2, BLK, 2 * HDIM), BF16)
    far_shape = jax.ShapeDtypeStruct((2, 2, BLK, 2 * HDIM), BF16)
    extras = [near_spec, near_spec, far_spec, far_spec]
    att, gq, dkv, dnear_p, dnear_m, dfar_p, dfar_m, pack = pl.pallas_call(
        attention_kernel,
        grid=(2,),
        out_shape=(
            jax.ShapeDtypeStruct(queries.shape, BF16),
            jax.ShapeDtypeStruct(queries.shape, BF16),
            jax.ShapeDtypeStruct(kv.shape, F32),
            near_shape,
            near_shape,
            far_shape,
            far_shape,
            far_shape,
        ),
        in_specs=[smem(), wide, pl.BlockSpec((2, 1, BLK, REP * HDIM), lambda g: (0, g, 0, 0)), pairs_spec] + extras,
        out_specs=[wide, wide, pairs_spec] + extras + [far_spec],
        cost_estimate=cost(8 * 10**9, 10 * 2**20),
        compiler_params=params(),
        name="attention",
    )(chosen, queries, grad_att, kv, near_p, near_m, first, second)

    near_p, near_m = lax.ppermute(dnear_p, ctx, line_down), lax.ppermute(dnear_m, ctx, line_up)
    rows = 2 * BLK

    def finish(keep, send):
        got = swap(send, "c")
        other = (keep[BLK:] + got[BLK:].astype(F32)).astype(BF16)
        back = swap(other, "x")
        return keep[:BLK] + got[:BLK].astype(F32) + back.astype(F32), other, back

    chunk = width // 2
    partial = (jax.ShapeDtypeStruct((rows, width), F32), jax.ShapeDtypeStruct((rows, width), BF16))
    out_parts = pl.pallas_call(
            output_kernel,
            grid=(width // chunk,),
            out_shape=partial,
            in_specs=[
                pl.BlockSpec((2, 2, rows, REP * HDIM), lambda k: (0, 0, 0, 0)),
                pl.BlockSpec((REP * HDIM, chunk), lambda k: (0, k)),
            ],
            out_specs=[pl.BlockSpec((rows, chunk), lambda k: (0, k))] * 2,
            cost_estimate=cost(2 * 10**9, 7 * 2**20),
            compiler_params=params(),
            name="output",
        )(att.reshape(2, 2, rows, REP * HDIM), o_weight)
    arrived = []
    far_p, far_m = trade(dfar_p, dfar_m, t, owner, True, arrived, (out_parts[1],), pack)
    total = out_parts[0] + swap(out_parts[1], "c").astype(F32)
    combined_back = swap(total[BLK:].astype(BF16), "x")
    combined = total[:BLK] + combined_back.astype(F32)
    combined = combined.astype(BF16)

    chunk = 256
    steps = width // chunk

    def fixed(shape):
        return pl.BlockSpec(shape, lambda k: (0,) * len(shape))

    part, kv_plain, kv_flipped = pl.pallas_call(
        query_part_kernel,
        grid=(steps,),
        out_shape=(
            jax.ShapeDtypeStruct((2, rows, width), F32),
            jax.ShapeDtypeStruct((width, 2 * HDIM), BF16),
            jax.ShapeDtypeStruct((width, 2 * HDIM), BF16),
        ),
        in_specs=[
            fixed((2, 2, rows, REP * HDIM)),
            pl.BlockSpec((chunk, (2 + REP) * HDIM), lambda k: (k, 0)),
            pl.BlockSpec((chunk, (2 + REP) * HDIM), lambda k: (steps - 1 - k, 0)),
        ],
        out_specs=(
            pl.BlockSpec((2, rows, chunk), lambda k: (0, 0, k)),
            pl.BlockSpec((chunk, 2 * HDIM), lambda k: (k, 0)),
            pl.BlockSpec((chunk, 2 * HDIM), lambda k: (k, 0)),
        ),
        cost_estimate=cost(3 * 10**9, 13 * 2**20),
        compiler_params=params(),
        name="query_part",
    )(after(gq, arrived[1]).reshape(2, 2, rows, REP * HDIM), weight, weight)

    chunk = width // 2
    key_shape = (2, 2, rows, 2 * HDIM)

    def sections(start):
        return [
            pl.BlockSpec((2, rows, chunk), lambda k: (0, 0, k + start)),
            pl.BlockSpec((chunk, 2 * HDIM), lambda k: (k + start, 0)),
            pl.BlockSpec((chunk, 2 * HDIM), lambda k: (k + start, 0)),
        ]

    key_parts = pl.pallas_call(
        key_part_kernel,
        grid=(2,),
        out_shape=partial,
        in_specs=[smem()]
        + [fixed(v) for v in (dkv.shape, near_shape.shape, near_shape.shape)]
        + [fixed(far_shape.shape)] * 2
        + sections(0),
        out_specs=[pl.BlockSpec((rows, chunk), lambda k: (0, k))] * 2,
        scratch_shapes=[pltpu.VMEM(key_shape, BF16)],
        cost_estimate=cost(5 * 10**8, 8 * 2**20),
        compiler_params=params(),
        name="key_part",
    )(chosen, dkv, near_p, near_m, after(far_p, combined_back), far_m, part, kv_plain, kv_flipped)
    grad_norm, _, _ = finish(*key_parts)

    u = hidden.astype(F32)
    inv_rms = lax.rsqrt(jnp.mean(u * u, axis=1, keepdims=True) + EPS)
    scaled = u * inv_rms
    grad_in = inv_rms * (grad_norm - scaled * jnp.mean(grad_norm * scaled, axis=1, keepdims=True))
    return (combined, grad_in.astype(BF16))


def split(count):
    inner = 1
    while (2 * inner) ** 2 <= count:
        inner *= 2
    return count // inner, inner


def solution(mesh):
    na, nb = split(mesh.shape["ctx"] // 2)
    grid = Mesh(mesh.devices.reshape(mesh.shape["groups"], na, nb, 2), ("x", "a", "b", "c"))
    return jax.shard_map(
        body,
        mesh=grid,
        in_specs=(
            P(("x", "a", "b", "c"), None),
            P(("a", "b", "c"), None),
            P(("a", "b", "c"), None),
            P(("a", "b", "c"), None),
            P("x"),
            P(("x", "a", "b", "c"), None),
        ),
        out_specs=(P(("x", "a", "b", "c"), None), P(("x", "a", "b", "c"), None)),
        check_vma=False,
    )
```
